512 devices in a mesh: rows: 32 (over y, z_hi, core), cols: 16 (over x, z_lo).
Axes of the slice: x: 4, y: 4, z: 16 (z_hi: 4, z_lo: 4; z = z_hi * 4 + z_lo), core: 2. Of those that a mesh axis runs over, the one named last changes fastest.
Arguments:
- a_vals: float32 [6144, 64, 896], P(('rows', 'cols')), may hold values from -0.1875 to 0.1875
- a_cols: int32 [6144, 14], P(('rows', 'cols')), may hold values from 0 to 6143, as said below
- a_count: int32 [6144], P(('rows', 'cols')), may hold values from 3 to 14, as said below
- p_vals: float32 [6144, 64, 320], P(('rows', 'cols')), may hold values from -3 to 3
- p_mask: int32 [6144, 5], P(('rows', 'cols')), may hold values 0 or 1
Outputs:
- coarse: float32 [512, 64, 704], P(('rows', 'cols'))
The draws below stay inside these ranges and needn't reach their ends.
Inputs may be any that keep to these rules, and one draw needn't show every extreme that they name: `a_cols`: each block row names 14 different block columns, the first its own; all lie among the 12 rows of its own slab or of the slab just before or after it, slabs taken in the order of rows, then cols; where those slabs exist, the second lies in the slab before and the third in the slab after. Slots at or after a_count of a block row are ignored; some block row has all 14 slots live.
All inputs are finite; a program needn't handle non-finite values. No bound on the sum of `p_mask` on one device may be relied on, other than what follows from the above.
Results may differ from the reference program's by a relative error of at most 0.0003.
Values sent between devices are 32-bit elements; how exact they have to be, the bound alone decides.
A program may use at most 128 MiB of HBM per device.

```python
import jax
import jax.numpy as jnp
from jax import lax

BLOCK = 64
KA = 14
PK = 5
FR = 12
AGGS = 512
FINE_BLOCKS = 6144


def draw_a_cols(key, part):
    fine_count = FINE_BLOCKS
    width_all = 3 * FR
    row_ids = jnp.arange(fine_count, dtype=jnp.int32)
    home = row_ids // FR
    candidate_ids = jnp.arange(width_all, dtype=jnp.int32)
    columns = (home[:, None] - 1) * FR + candidate_ids[None, :]
    scores = jax.random.randint(jax.random.fold_in(key, 11), (fine_count, width_all), 0, 1 << 20, dtype=jnp.int32)
    scores = scores * width_all + candidate_ids[None, :]
    lower_pick = jax.random.randint(jax.random.fold_in(key, 12), (fine_count, 1), 0, FR, dtype=jnp.int32)
    upper_pick = jax.random.randint(jax.random.fold_in(key, 13), (fine_count, 1), 0, FR, dtype=jnp.int32) + 2 * FR
    scores = jnp.where(candidate_ids[None, :] == lower_pick, -2, scores)
    scores = jnp.where(candidate_ids[None, :] == upper_pick, -1, scores)
    invalid = (columns < 0) | (columns >= fine_count)
    scores = jnp.where(invalid, scores + (1 << 30), scores)
    scores = jnp.where(columns == row_ids[:, None], -3, scores)
    order = jnp.argsort(scores, axis=1, stable=True)[:, :KA].astype(jnp.int32)
    return ((home[:, None] - 1) * FR + order).astype(jnp.int32)


def draw_a_count(key, part):
    fine_count = FINE_BLOCKS
    group_count = FINE_BLOCKS // FR
    low_limit = max(3, KA // 2)
    limits = jax.random.randint(jax.random.fold_in(key, 21), (group_count,), low_limit, KA + 1, dtype=jnp.int32)
    row_limit = jnp.repeat(limits, FR)
    raw_bits = jax.random.randint(jax.random.fold_in(key, 22), (fine_count,), 0, 1 << 20, dtype=jnp.int32)
    counts = 3 + raw_bits % (row_limit - 2)
    chosen = jax.random.randint(jax.random.fold_in(key, 23), (), 0, fine_count, dtype=jnp.int32)
    return jnp.where(jnp.arange(fine_count, dtype=jnp.int32) == chosen, KA, counts).astype(jnp.int32)


def set_ends(entries, stream_key, smallest, top_value):
    spot = [jax.random.randint(jax.random.fold_in(stream_key, axis), (), 0, length) for axis, length in enumerate(entries.shape)]
    main_axis = entries.shape.index(max(entries.shape))
    neighbour = spot[:main_axis] + [(spot[main_axis] + 1) % entries.shape[main_axis]] + spot[main_axis + 1:]
    return entries.at[tuple(spot)].set(smallest).at[tuple(neighbour)].set(top_value)


def shard_levels(rng, dims, split, least, largest):
    def one(position, parts):
        steps = jax.random.uniform(jax.random.fold_in(jax.random.fold_in(rng, 6), position), (parts,), jnp.float32, least / len(split), largest / len(split))
        return jnp.repeat(jnp.exp(steps), dims[position] // parts).reshape((-1,) + (1,) * (len(dims) - position - 1))

    factor_of = one(*split[0])
    for cut in split[1:]:
        factor_of = factor_of * one(*cut)
    return factor_of


def centred(own_key, shape, width, most, pieces=(), kind=jnp.bfloat16):
    drawn = width * jax.random.normal(own_key, shape, jnp.float32)
    if pieces:
        drawn = drawn * shard_levels(own_key, shape, pieces, -0.22, 0.18)
    return jnp.clip(drawn, -most, most).astype(kind)


def setup_inputs(seed: int = 0) -> dict:
    seeds = jax.random.split(jax.random.key(seed), 6)
    a_vals = centred(seeds[0], (FINE_BLOCKS, BLOCK, KA * BLOCK), (KA * BLOCK) ** -0.5, 0.1875, ((0, 512),), jnp.float32)
    a_cols = draw_a_cols(jax.random.fold_in(seeds[5], 71), 0)
    a_count = draw_a_count(jax.random.fold_in(seeds[5], 71), 0)
    p_vals = centred(seeds[3], (FINE_BLOCKS, BLOCK, PK * BLOCK), 0.2, 3.0, ((0, 512),), jnp.float32)
    p_mask = set_ends((jax.random.randint(seeds[4], (FINE_BLOCKS, PK), 0, 4) < 3).astype(jnp.int32), jax.random.fold_in(seeds[4], 1), 0, 1)
    return {"a_vals": a_vals, "a_cols": a_cols, "a_count": a_count, "p_vals": p_vals, "p_mask": p_mask}


FULL_PRECISION = lax.Precision.HIGHEST


def shift_groups(values, amount):
    if amount == 0:
        return values
    filler = jnp.zeros((abs(amount),) + values.shape[1:], jnp.float32)
    if amount > 0:
        return jnp.concatenate([filler, values[:-amount]], axis=0)
    return jnp.concatenate([values[-amount:], filler], axis=0)


def reference(a_vals, a_cols, a_count, p_vals, p_mask):
    fine_count = FINE_BLOCKS
    block_size = BLOCK
    row_ids = jnp.arange(fine_count, dtype=jnp.int32)
    home = row_ids // FR
    slot_ids = jnp.arange(PK, dtype=jnp.int32)
    target = home[:, None] + slot_ids[None, :] - 2
    inside = ((target >= 0) & (target < AGGS)).astype(jnp.float32)
    keep_mask = p_mask.astype(jnp.float32) * inside
    pblocks = p_vals.reshape(fine_count, block_size, PK, block_size) * keep_mask[:, None, :, None]
    pflat = pblocks.reshape(fine_count, block_size, PK * block_size)
    a_slots = jnp.arange(KA, dtype=jnp.int32)
    side_ids = jnp.arange(3, dtype=jnp.int32)

    def one_row(items):
        row_index, row_matrix, row_cols, row_count = items
        gathered = jnp.take(pflat, row_cols, axis=0)
        matrix_rows = row_matrix.reshape(block_size, KA, block_size)
        products = jnp.einsum('fkg,kgc->kfc', matrix_rows, gathered, precision=FULL_PRECISION)
        side_index = row_cols // FR - row_index // FR + 1
        weights = ((a_slots < row_count)[:, None] & (side_index[:, None] == side_ids[None, :])).astype(jnp.float32)
        mixed = jnp.einsum('kd,kfc->dfc', weights, products, precision=FULL_PRECISION)
        bands = jnp.zeros((block_size, (PK + 2) * block_size), jnp.float32)
        for side in range(3):
            bands = bands + jnp.pad(mixed[side], ((0, 0), (side * block_size, (2 - side) * block_size)))
        return bands

    ap = lax.map(one_row, (row_ids, a_vals, a_cols, a_count))

    def one_group(group_index):
        first = (group_index * FR).astype(jnp.int32)
        p_slice = lax.dynamic_slice_in_dim(pblocks, first, FR, axis=0)
        ap_slice = lax.dynamic_slice_in_dim(ap, first, FR, axis=0)
        terms = jnp.einsum('ifsc,ifq->scq', p_slice, ap_slice, precision=FULL_PRECISION)
        spread = [jnp.pad(terms[s], ((0, 0), ((PK - 1 - s) * block_size, s * block_size))) for s in range(PK)]
        return jnp.stack(spread)

    groups = lax.map(one_group, jnp.arange(AGGS, dtype=jnp.int32))
    total = jnp.zeros((AGGS, block_size, (PK + 6) * block_size), jnp.float32)
    for s in range(PK):
        total = total + shift_groups(groups[:, s], s - 2)
    return total
```

```python
import jax
import jax.numpy as jnp
from jax import lax
from jax.sharding import PartitionSpec as P

FULL_PRECISION = lax.Precision.HIGHEST


def from_behind(array, axis, by):
    count = lax.axis_size(axis)
    pairs = [(i, i + by) for i in range(count) if 0 <= i + by < count]
    return lax.ppermute(array, axis, pairs)


def mm(a, b):
    return jnp.dot(a, b, precision=FULL_PRECISION, preferred_element_type=jnp.float32)


def shards(a_vals, a_cols, a_count, p_vals, p_mask):
    rows_here = a_cols.shape[0]
    slot_count = a_cols.shape[1]
    block_size = a_vals.shape[1]
    prol_slots = p_mask.shape[1]
    group_total = lax.axis_size("rows") * lax.axis_size("cols")
    position = lax.axis_index("rows") * lax.axis_size("cols") + lax.axis_index("cols")
    slot_ids = jnp.arange(prol_slots, dtype=jnp.int32)
    target = position + slot_ids - 2
    inside = ((target >= 0) & (target < group_total)).astype(jnp.float32)
    keep_mask = p_mask.astype(jnp.float32) * inside[None, :]
    pblocks = (
        p_vals.reshape(rows_here, block_size, prol_slots, block_size) * keep_mask[:, None, :, None]
    )
    pflat = pblocks.reshape(rows_here, block_size, prol_slots * block_size)
    lower_rows = from_behind(pflat, ("rows", "cols"), 1)
    upper_rows = from_behind(pflat, ("rows", "cols"), -1)

    local_cols = a_cols - (position - 1) * rows_here
    live_mask = jnp.arange(slot_count, dtype=jnp.int32)[None, :] < a_count[:, None]
    col_ids = jnp.arange(3 * rows_here, dtype=jnp.int32)
    onehot = (live_mask[:, :, None] & (local_cols[:, :, None] == col_ids[None, None, :])).astype(
        jnp.float32
    )
    matrix_rows = a_vals.reshape(rows_here, block_size, slot_count, block_size)
    dense = jnp.einsum("ifkg,ikn->ifng", matrix_rows, onehot, precision=FULL_PRECISION)
    dense = dense.reshape(rows_here * block_size, 3 * rows_here * block_size)
    span = rows_here * block_size
    width = prol_slots * block_size
    own = mm(dense[:, span : 2 * span], pflat.reshape(span, width))
    low = mm(dense[:, :span], lower_rows.reshape(span, width))
    high = mm(dense[:, 2 * span :], upper_rows.reshape(span, width))
    ap_rows = (
        jnp.pad(low, ((0, 0), (0, 2 * block_size)))
        + jnp.pad(own, ((0, 0), (block_size, block_size)))
        + jnp.pad(high, ((0, 0), (2 * block_size, 0)))
    )
    terms = lax.dot_general(
        pflat.reshape(span, width),
        ap_rows,
        (((0,), (0,)), ((), ())),
        precision=FULL_PRECISION,
        preferred_element_type=jnp.float32,
    ).reshape(prol_slots, block_size, (prol_slots + 2) * block_size)

    def spread(s, block):
        return jnp.pad(block, ((0, 0), ((prol_slots - 1 - s) * block_size, s * block_size)))

    result = spread(2, terms[2])
    result = result + spread(3, from_behind(terms[3], ("rows", "cols"), 1))
    result = result + spread(4, from_behind(terms[4], ("rows", "cols"), 2))
    result = result + spread(1, from_behind(terms[1], ("rows", "cols"), -1))
    result = result + spread(0, from_behind(terms[0], ("rows", "cols"), -2))
    return result.reshape(1, block_size, (prol_slots + 6) * block_size)


def solution(mesh):
    in_specs = (
        P(("rows", "cols"), None, None),
        P(("rows", "cols"), None),
        P(("rows", "cols")),
        P(("rows", "cols"), None, None),
        P(("rows", "cols"), None),
    )
    out_specs = P(("rows", "cols"), None, None)
    return jax.shard_map(shards, mesh=mesh, in_specs=in_specs, out_specs=out_specs, check_vma=False)
```

```python
import jax
import jax.numpy as jnp
from jax import lax
from jax.sharding import PartitionSpec as P

FULL_PRECISION = lax.Precision.HIGHEST


def from_behind(array, axis, by):
    count = lax.axis_size(axis)
    pairs = [(i, i + by) for i in range(count) if 0 <= i + by < count]
    return lax.ppermute(array, axis, pairs)


def mm(a, b):
    return jnp.dot(a, b, precision=FULL_PRECISION, preferred_element_type=jnp.float32)


def shards(a_vals, a_cols, a_count, p_vals, p_mask):
    rows_here = a_cols.shape[0]
    slot_count = a_cols.shape[1]
    block_size = a_vals.shape[1]
    prol_slots = p_mask.shape[1]
    group_total = lax.axis_size("rows") * lax.axis_size("cols")
    position = lax.axis_index("rows") * lax.axis_size("cols") + lax.axis_index("cols")
    slot_ids = jnp.arange(prol_slots, dtype=jnp.int32)
    target = position + slot_ids - 2
    inside = ((target >= 0) & (target < group_total)).astype(jnp.float32)
    keep_mask = p_mask.astype(jnp.float32) * inside[None, :]
    pblocks = (
        p_vals.reshape(rows_here, block_size, prol_slots, block_size) * keep_mask[:, None, :, None]
    )
    pflat = pblocks.reshape(rows_here, block_size, prol_slots * block_size)
    lower_rows = from_behind(pflat, ("rows", "cols"), 1)
    upper_rows = from_behind(pflat, ("rows", "cols"), -1)

    local_cols = a_cols - (position - 1) * rows_here
    live_mask = jnp.arange(slot_count, dtype=jnp.int32)[None, :] < a_count[:, None]
    col_ids = jnp.arange(3 * rows_here, dtype=jnp.int32)
    onehot = (live_mask[:, :, None] & (local_cols[:, :, None] == col_ids[None, None, :])).astype(
        jnp.float32
    ).reshape(rows_here * slot_count, 3 * rows_here)
    span = rows_here * block_size
    width = prol_slots * block_size
    wide = (prol_slots + 2) * block_size
    flat_len = block_size * wide
    matrix_rows = a_vals.reshape(rows_here, block_size, slot_count * block_size)

    def gathered(weights, p_rows):
        picked = mm(weights, p_rows.reshape(p_rows.shape[0], flat_len))
        return picked.reshape(rows_here, slot_count * block_size, wide)

    def times_a(picked):
        return jnp.einsum("ifK,iKq->ifq", matrix_rows, picked, precision=FULL_PRECISION)

    own_sh = jnp.pad(pflat, ((0, 0), (0, 0), (block_size, block_size)))
    ap_own = times_a(gathered(onehot[:, rows_here : 2 * rows_here], own_sh))
    side_sh = jnp.concatenate(
        [
            jnp.pad(lower_rows, ((0, 0), (0, 0), (0, 2 * block_size))),
            jnp.pad(upper_rows, ((0, 0), (0, 0), (2 * block_size, 0))),
        ],
        axis=0,
    )
    side_weights = jnp.concatenate([onehot[:, :rows_here], onehot[:, 2 * rows_here :]], axis=1)
    ap_rows = (ap_own + times_a(gathered(side_weights, side_sh))).reshape(span, wide)
    terms = lax.dot_general(
        pflat.reshape(span, width),
        ap_rows,
        (((0,), (0,)), ((), ())),
        precision=FULL_PRECISION,
        preferred_element_type=jnp.float32,
    ).reshape(prol_slots, block_size, (prol_slots + 2) * block_size)

    def spread(s, block):
        return jnp.pad(block, ((0, 0), ((prol_slots - 1 - s) * block_size, s * block_size)))

    result = spread(2, terms[2])
    result = result + spread(3, from_behind(terms[3], ("rows", "cols"), 1))
    result = result + spread(4, from_behind(terms[4], ("rows", "cols"), 2))
    result = result + spread(1, from_behind(terms[1], ("rows", "cols"), -1))
    result = result + spread(0, from_behind(terms[0], ("rows", "cols"), -2))
    return result.reshape(1, block_size, (prol_slots + 6) * block_size)


def solution(mesh):
    in_specs = (
        P(("rows", "cols"), None, None),
        P(("rows", "cols"), None),
        P(("rows", "cols")),
        P(("rows", "cols"), None, None),
        P(("rows", "cols"), None),
    )
    out_specs = P(("rows", "cols"), None, None)
    return jax.shard_map(shards, mesh=mesh, in_specs=in_specs, out_specs=out_specs, check_vma=False)
```

```python
import jax
import jax.numpy as jnp
from jax import lax
from jax.experimental import pallas as pl
from jax.experimental.pallas import tpu as pltpu
from jax.sharding import PartitionSpec as P

MATMUL_PRECISION = lax.Precision.HIGH


def from_behind(array, axis, by):
    count = lax.axis_size(axis)
    pairs = [(i, i + by) for i in range(count) if 0 <= i + by < count]
    return lax.ppermute(array, axis, pairs)


def mm(a, b):
    return jnp.dot(a, b, precision=MATMUL_PRECISION, preferred_element_type=jnp.float32)


def dense_kernel(slot_ref, a_ref, out_ref):
    sides, rows_here, block_size, span = out_ref.shape
    per_side = span // block_size
    lanes = 2 * block_size
    left = lax.broadcasted_iota(jnp.int32, (block_size, lanes), 1) < block_size

    def one_row(i, carry):
        for d in range(sides):
            for m in range(per_side // 2):
                halves = []
                for h in range(2):
                    slot = slot_ref[(i * sides + d) * per_side + 2 * m + h]
                    safe = jnp.maximum(slot, 0)
                    start = pl.multiple_of((safe // 2) * lanes, lanes)
                    tile = a_ref[i, :, pl.ds(start, lanes)]
                    rolled = pltpu.roll(tile, block_size, 1)
                    turn = (safe % 2) != h
                    picked = jnp.where(turn, rolled, tile)
                    halves.append(jnp.where(slot >= 0, picked, jnp.zeros_like(picked)))
                out_ref[d, i, :, m * lanes : (m + 1) * lanes] = jnp.where(left, halves[0], halves[1])
        return carry

    lax.fori_loop(0, rows_here, one_row, 0)


def dense_sides(slot_table, a_vals):
    rows_here, block_size, _ = a_vals.shape
    span = rows_here * block_size
    return pl.pallas_call(
        dense_kernel,
        out_shape=jax.ShapeDtypeStruct((3, rows_here, block_size, span), jnp.float32),
        in_specs=[
            pl.BlockSpec(memory_space=pltpu.SMEM),
            pl.BlockSpec(memory_space=pltpu.VMEM),
        ],
        out_specs=pl.BlockSpec(memory_space=pltpu.VMEM),
    )(slot_table, a_vals)


def shards(a_vals, a_cols, a_count, p_vals, p_mask):
    rows_here = a_cols.shape[0]
    slot_count = a_cols.shape[1]
    block_size = a_vals.shape[1]
    prol_slots = p_mask.shape[1]
    group_total = lax.axis_size("rows") * lax.axis_size("cols")
    position = lax.axis_index("rows") * lax.axis_size("cols") + lax.axis_index("cols")
    slot_ids = jnp.arange(prol_slots, dtype=jnp.int32)
    target = position + slot_ids - 2
    inside = ((target >= 0) & (target < group_total)).astype(jnp.float32)
    keep_mask = p_mask.astype(jnp.float32) * inside[None, :]
    pblocks = (
        p_vals.reshape(rows_here, block_size, prol_slots, block_size) * keep_mask[:, None, :, None]
    )
    pflat = pblocks.reshape(rows_here, block_size, prol_slots * block_size)
    lower_rows = from_behind(pflat, ("rows", "cols"), 1)
    upper_rows = from_behind(pflat, ("rows", "cols"), -1)

    local_cols = a_cols - (position - 1) * rows_here
    live_mask = jnp.arange(slot_count, dtype=jnp.int32)[None, :] < a_count[:, None]
    col_ids = jnp.arange(3 * rows_here, dtype=jnp.int32)
    hit = live_mask[:, :, None] & (local_cols[:, :, None] == col_ids[None, None, :])
    slot_numbers = jnp.arange(1, slot_count + 1, dtype=jnp.int32)[None, :, None]
    slot_table = (jnp.sum(jnp.where(hit, slot_numbers, 0), axis=1) - 1).reshape(-1)
    span = rows_here * block_size
    width = prol_slots * block_size
    dense = dense_sides(slot_table, a_vals).reshape(3, span, span)
    own = mm(dense[1], pflat.reshape(span, width))
    low = mm(dense[0], lower_rows.reshape(span, width))
    high = mm(dense[2], upper_rows.reshape(span, width))
    ap_rows = (
        jnp.pad(low, ((0, 0), (0, 2 * block_size)))
        + jnp.pad(own, ((0, 0), (block_size, block_size)))
        + jnp.pad(high, ((0, 0), (2 * block_size, 0)))
    )
    terms = lax.dot_general(
        pflat.reshape(span, width),
        ap_rows,
        (((0,), (0,)), ((), ())),
        precision=MATMUL_PRECISION,
        preferred_element_type=jnp.float32,
    ).reshape(prol_slots, block_size, (prol_slots + 2) * block_size)

    def spread(s, block):
        return jnp.pad(block, ((0, 0), ((prol_slots - 1 - s) * block_size, s * block_size)))

    result = spread(2, terms[2])
    result = result + spread(3, from_behind(terms[3], ("rows", "cols"), 1))
    result = result + spread(4, from_behind(terms[4], ("rows", "cols"), 2))
    result = result + spread(1, from_behind(terms[1], ("rows", "cols"), -1))
    result = result + spread(0, from_behind(terms[0], ("rows", "cols"), -2))
    return result.reshape(1, block_size, (prol_slots + 6) * block_size)


def solution(mesh):
    in_specs = (
        P(("rows", "cols"), None, None),
        P(("rows", "cols"), None),
        P(("rows", "cols")),
        P(("rows", "cols"), None, None),
        P(("rows", "cols"), None),
    )
    out_specs = P(("rows", "cols"), None, None)
    return jax.shard_map(shards, mesh=mesh, in_specs=in_specs, out_specs=out_specs, check_vma=False)
```

```python
import jax
import jax.numpy as jnp
from jax import lax
from jax.experimental import pallas as pl
from jax.experimental.pallas import tpu as pltpu
from jax.sharding import PartitionSpec as P

MATMUL_PRECISION = lax.Precision.HIGH


def from_behind(array, axis, by):
    count = lax.axis_size(axis)
    pairs = [(i, i + by) for i in range(count) if 0 <= i + by < count]
    return lax.ppermute(array, axis, pairs)


def mm(a, b):
    return jnp.dot(a, b, precision=MATMUL_PRECISION, preferred_element_type=jnp.float32)


def dense_kernel(slot_ref, a_ref, out_ref):
    sides, rows_here, block_size, span = out_ref.shape
    per_side = span // block_size
    lanes = 2 * block_size
    left = lax.broadcasted_iota(jnp.int32, (block_size, lanes), 1) < block_size

    def one_row(i, carry):
        for d in range(sides):
            for m in range(per_side // 2):
                halves = []
                for h in range(2):
                    slot = slot_ref[(i * sides + d) * per_side + 2 * m + h]
                    safe = jnp.maximum(slot, 0)
                    start = pl.multiple_of((safe // 2) * lanes, lanes)
                    tile = a_ref[i, :, pl.ds(start, lanes)]
                    rolled = pltpu.roll(tile, block_size, 1)
                    turn = (safe % 2) != h
                    picked = jnp.where(turn, rolled, tile)
                    halves.append(jnp.where(slot >= 0, picked, jnp.zeros_like(picked)))
                out_ref[d, i, :, m * lanes : (m + 1) * lanes] = jnp.where(left, halves[0], halves[1])
        return carry

    lax.fori_loop(0, rows_here, one_row, 0)


def dense_sides(slot_table, a_vals):
    rows_here, block_size, _ = a_vals.shape
    span = rows_here * block_size
    return pl.pallas_call(
        dense_kernel,
        out_shape=jax.ShapeDtypeStruct((3, rows_here, block_size, span), jnp.float32),
        in_specs=[
            pl.BlockSpec(memory_space=pltpu.SMEM),
            pl.BlockSpec(memory_space=pltpu.VMEM),
        ],
        out_specs=pl.BlockSpec(memory_space=pltpu.VMEM),
    )(slot_table, a_vals)


def shards(a_vals, a_cols, a_count, p_vals, p_mask):
    rows_here = a_cols.shape[0]
    slot_count = a_cols.shape[1]
    block_size = a_vals.shape[1]
    prol_slots = p_mask.shape[1]
    group_total = lax.axis_size("rows") * lax.axis_size("cols")
    position = lax.axis_index("rows") * lax.axis_size("cols") + lax.axis_index("cols")
    flat_axis = ("rows", "cols")
    lower_raw = from_behind(p_vals, flat_axis, 1)
    upper_raw = from_behind(p_vals, flat_axis, -1)
    lower_mask = from_behind(p_mask, flat_axis, 1)
    upper_mask = from_behind(p_mask, flat_axis, -1)
    slot_ids = jnp.arange(prol_slots, dtype=jnp.int32)
    span = rows_here * block_size
    width = prol_slots * block_size

    def masked(values, mask, owner):
        target = owner + slot_ids - 2
        inside = ((target >= 0) & (target < group_total)).astype(jnp.float32)
        keep = mask.astype(jnp.float32) * inside[None, :]
        blocks = values.reshape(rows_here, block_size, prol_slots, block_size) * keep[:, None, :, None]
        return blocks.reshape(span, width)

    p_own = masked(p_vals, p_mask, position)

    local_cols = a_cols - (position - 1) * rows_here
    live_mask = jnp.arange(slot_count, dtype=jnp.int32)[None, :] < a_count[:, None]
    col_ids = jnp.arange(3 * rows_here, dtype=jnp.int32)
    hit = live_mask[:, :, None] & (local_cols[:, :, None] == col_ids[None, None, :])
    slot_numbers = jnp.arange(1, slot_count + 1, dtype=jnp.int32)[None, :, None]
    slot_table = (jnp.sum(jnp.where(hit, slot_numbers, 0), axis=1) - 1).reshape(-1)
    dense = dense_sides(slot_table, a_vals).reshape(3, span, span)

    def pt_times(side):
        return lax.dot_general(
            p_own,
            dense[side],
            (((0,), (0,)), ((), ())),
            precision=MATMUL_PRECISION,
            preferred_element_type=jnp.float32,
        )

    t_own = mm(pt_times(1), p_own)
    t_low = mm(pt_times(0), masked(lower_raw, lower_mask, position - 1))
    t_high = mm(pt_times(2), masked(upper_raw, upper_mask, position + 1))
    terms = (
        jnp.pad(t_low, ((0, 0), (0, 2 * block_size)))
        + jnp.pad(t_own, ((0, 0), (block_size, block_size)))
        + jnp.pad(t_high, ((0, 0), (2 * block_size, 0)))
    ).reshape(prol_slots, block_size, (prol_slots + 2) * block_size)

    def spread(s, block):
        return jnp.pad(block, ((0, 0), ((prol_slots - 1 - s) * block_size, s * block_size)))

    result = spread(2, terms[2])
    result = result + spread(3, from_behind(terms[3], flat_axis, 1))
    result = result + spread(4, from_behind(terms[4], flat_axis, 2))
    result = result + spread(1, from_behind(terms[1], flat_axis, -1))
    result = result + spread(0, from_behind(terms[0], flat_axis, -2))
    return result.reshape(1, block_size, (prol_slots + 6) * block_size)


def solution(mesh):
    in_specs = (
        P(("rows", "cols"), None, None),
        P(("rows", "cols"), None),
        P(("rows", "cols")),
        P(("rows", "cols"), None, None),
        P(("rows", "cols"), None),
    )
    out_specs = P(("rows", "cols"), None, None)
    return jax.shard_map(shards, mesh=mesh, in_specs=in_specs, out_specs=out_specs, check_vma=False)
```

```python
import jax
import jax.numpy as jnp
from jax import lax
from jax.experimental import pallas as pl
from jax.experimental.pallas import tpu as pltpu
from jax.sharding import PartitionSpec as P

MATMUL_PRECISION = lax.Precision.HIGH


def from_behind(array, axis, by):
    count = lax.axis_size(axis)
    pairs = [(i, i + by) for i in range(count) if 0 <= i + by < count]
    return lax.ppermute(array, axis, pairs)


def mm(a, b):
    return jnp.dot(a, b, precision=MATMUL_PRECISION, preferred_element_type=jnp.float32)


def dense_kernel(slot_ref, a_ref, *out_refs):
    sides = len(out_refs)
    rows_here, block_size, span = out_refs[0].shape
    per_side = span // block_size
    lanes = 2 * block_size
    left = lax.broadcasted_iota(jnp.int32, (block_size, lanes), 1) < block_size

    def one_row(i, carry):
        for d in range(sides):
            for m in range(per_side // 2):
                halves = []
                for h in range(2):
                    slot = slot_ref[(i * sides + d) * per_side + 2 * m + h]
                    safe = jnp.maximum(slot, 0)
                    start = pl.multiple_of((safe // 2) * lanes, lanes)
                    tile = a_ref[i, :, pl.ds(start, lanes)]
                    rolled = pltpu.roll(tile, block_size, 1)
                    turn = (safe % 2) != h
                    picked = jnp.where(turn, rolled, tile)
                    halves.append(jnp.where(slot >= 0, picked, jnp.zeros_like(picked)))
                out_refs[d][i, :, m * lanes : (m + 1) * lanes] = jnp.where(left, halves[0], halves[1])
        return carry

    lax.fori_loop(0, rows_here, one_row, 0)


def dense_sides(slot_table, a_vals):
    rows_here, block_size, _ = a_vals.shape
    span = rows_here * block_size
    return pl.pallas_call(
        dense_kernel,
        out_shape=[jax.ShapeDtypeStruct((rows_here, block_size, span), jnp.float32)] * 3,
        in_specs=[
            pl.BlockSpec(memory_space=pltpu.SMEM),
            pl.BlockSpec(memory_space=pltpu.VMEM),
        ],
        out_specs=[pl.BlockSpec(memory_space=pltpu.VMEM)] * 3,
    )(slot_table, a_vals)


def shards(a_vals, a_cols, a_count, p_vals, p_mask):
    rows_here = a_cols.shape[0]
    slot_count = a_cols.shape[1]
    block_size = a_vals.shape[1]
    prol_slots = p_mask.shape[1]
    group_total = lax.axis_size("rows") * lax.axis_size("cols")
    position = lax.axis_index("rows") * lax.axis_size("cols") + lax.axis_index("cols")
    flat_axis = ("rows", "cols")
    slot_ids = jnp.arange(prol_slots, dtype=jnp.int32)
    target = position + slot_ids - 2
    inside = ((target >= 0) & (target < group_total)).astype(jnp.float32)
    keep = jnp.repeat(p_mask.astype(jnp.float32) * inside[None, :], block_size, axis=1)
    pflat = p_vals * keep[:, None, :]
    lower_rows = from_behind(pflat, flat_axis, 1)
    upper_rows = from_behind(pflat, flat_axis, -1)
    span = rows_here * block_size
    width = prol_slots * block_size
    p_own = pflat.reshape(span, width)

    local_cols = a_cols - (position - 1) * rows_here
    live_mask = jnp.arange(slot_count, dtype=jnp.int32)[None, :] < a_count[:, None]
    col_ids = jnp.arange(3 * rows_here, dtype=jnp.int32)
    hit = live_mask[:, :, None] & (local_cols[:, :, None] == col_ids[None, None, :])
    slot_numbers = jnp.arange(1, slot_count + 1, dtype=jnp.int32)[None, :, None]
    slot_table = (jnp.sum(jnp.where(hit, slot_numbers, 0), axis=1) - 1).reshape(-1)
    dense = [side.reshape(span, span) for side in dense_sides(slot_table, a_vals)]

    def pt_times(side):
        return lax.dot_general(
            p_own,
            dense[side],
            (((0,), (0,)), ((), ())),
            precision=MATMUL_PRECISION,
            preferred_element_type=jnp.float32,
        )

    t_own = mm(pt_times(1), p_own)
    t_low = mm(pt_times(0), lower_rows.reshape(span, width))
    t_high = mm(pt_times(2), upper_rows.reshape(span, width))
    terms = (
        jnp.pad(t_low, ((0, 0), (0, 2 * block_size)))
        + jnp.pad(t_own, ((0, 0), (block_size, block_size)))
        + jnp.pad(t_high, ((0, 0), (2 * block_size, 0)))
    ).reshape(prol_slots, block_size, (prol_slots + 2) * block_size)

    def spread(s, block):
        return jnp.pad(block, ((0, 0), ((prol_slots - 1 - s) * block_size, s * block_size)))

    result = spread(2, terms[2])
    result = result + spread(3, from_behind(terms[3], flat_axis, 1))
    result = result + spread(4, from_behind(terms[4], flat_axis, 2))
    result = result + spread(1, from_behind(terms[1], flat_axis, -1))
    result = result + spread(0, from_behind(terms[0], flat_axis, -2))
    return result.reshape(1, block_size, (prol_slots + 6) * block_size)


def solution(mesh):
    in_specs = (
        P(("rows", "cols"), None, None),
        P(("rows", "cols"), None),
        P(("rows", "cols")),
        P(("rows", "cols"), None, None),
        P(("rows", "cols"), None),
    )
    out_specs = P(("rows", "cols"), None, None)
    return jax.shard_map(shards, mesh=mesh, in_specs=in_specs, out_specs=out_specs, check_vma=False)
```

```python
import jax
import jax.numpy as jnp
from jax import lax
from jax.experimental import pallas as pl
from jax.experimental.pallas import tpu as pltpu
from jax.sharding import PartitionSpec as P

MATMUL_PRECISION = lax.Precision.HIGH


def from_behind(array, axis, by):
    count = lax.axis_size(axis)
    pairs = [(i, i + by) for i in range(count) if 0 <= i + by < count]
    return lax.ppermute(array, axis, pairs)


def mm(a, b):
    return jnp.dot(a, b, precision=MATMUL_PRECISION, preferred_element_type=jnp.float32)


def dense_kernel(slot_ref, a_ref, *out_refs):
    sides = len(out_refs)
    rows_here, block_size, span = out_refs[0].shape
    per_side = span // block_size
    lanes = 2 * block_size
    left = lax.broadcasted_iota(jnp.int32, (block_size, lanes), 1) < block_size

    def one_row(i, carry):
        for d in range(sides):
            for m in range(per_side // 2):
                halves = []
                for h in range(2):
                    slot = slot_ref[(i * sides + d) * per_side + 2 * m + h]
                    safe = jnp.maximum(slot, 0)
                    start = pl.multiple_of((safe // 2) * lanes, lanes)
                    tile = a_ref[i, :, pl.ds(start, lanes)]
                    rolled = pltpu.roll(tile, block_size, 1)
                    turn = (safe % 2) != h
                    picked = jnp.where(turn, rolled, tile)
                    halves.append(jnp.where(slot >= 0, picked, jnp.zeros_like(picked)))
                out_refs[d][i, :, m * lanes : (m + 1) * lanes] = jnp.where(left, halves[0], halves[1])
        return carry

    lax.fori_loop(0, rows_here, one_row, 0)


def dense_sides(slot_table, a_vals):
    rows_here, block_size, _ = a_vals.shape
    span = rows_here * block_size
    return pl.pallas_call(
        dense_kernel,
        out_shape=[jax.ShapeDtypeStruct((rows_here, block_size, span), jnp.float32)] * 3,
        in_specs=[
            pl.BlockSpec(memory_space=pltpu.SMEM),
            pl.BlockSpec(memory_space=pltpu.VMEM),
        ],
        out_specs=[pl.BlockSpec(memory_space=pltpu.VMEM)] * 3,
    )(slot_table, a_vals)


def exchange_kernel(terms_ref, out_ref, recv, send_sem, recv_sem):
    col_count = lax.axis_size("cols")
    total = lax.axis_size("rows") * col_count
    me = lax.axis_index("rows") * col_count + lax.axis_index("cols")
    centre = terms_ref.shape[0] // 2
    shifts = [s - centre for s in range(terms_ref.shape[0]) if s != centre]

    def mesh_id(pos):
        return (pos // col_count, pos % col_count)

    barrier = pltpu.get_barrier_semaphore()
    for shift in shifts:
        @pl.when((me + shift >= 0) & (me + shift < total))
        def _():
            pl.semaphore_signal(
                barrier, 1, device_id=mesh_id(me + shift), device_id_type=pl.DeviceIdType.MESH
            )

    peers = 0
    for shift in shifts:
        peers = peers + ((me + shift >= 0) & (me + shift < total)).astype(jnp.int32)
    pl.semaphore_wait(barrier, peers)

    copies = []
    for u, shift in enumerate(shifts):
        copy = pltpu.make_async_remote_copy(
            src_ref=terms_ref.at[shift + centre],
            dst_ref=recv.at[u],
            send_sem=send_sem.at[u],
            recv_sem=recv_sem.at[u],
            device_id=mesh_id(me + shift),
            device_id_type=pl.DeviceIdType.MESH,
        )
        copies.append(copy)

        @pl.when((me + shift >= 0) & (me + shift < total))
        def _():
            copy.start()

    for u, shift in enumerate(shifts):
        sends = (me + shift >= 0) & (me + shift < total)
        gets = (me - shift >= 0) & (me - shift < total)

        @pl.when(sends)
        def _():
            copies[u].wait_send()

        @pl.when(gets)
        def _():
            copies[u].wait_recv()
            out_ref[u] = recv[u]

        @pl.when(jnp.logical_not(gets))
        def _():
            out_ref[u] = jnp.zeros(out_ref.shape[1:], out_ref.dtype)


def exchange(terms):
    parts, block_size, wide = terms.shape
    return pl.pallas_call(
        exchange_kernel,
        out_shape=jax.ShapeDtypeStruct((parts - 1, block_size, wide), jnp.float32),
        in_specs=[pl.BlockSpec(memory_space=pltpu.VMEM)],
        out_specs=pl.BlockSpec(memory_space=pltpu.VMEM),
        scratch_shapes=[
            pltpu.VMEM((parts - 1, block_size, wide), jnp.float32),
            pltpu.SemaphoreType.DMA((parts - 1,)),
            pltpu.SemaphoreType.DMA((parts - 1,)),
        ],
        compiler_params=pltpu.CompilerParams(collective_id=0, has_side_effects=True),
    )(terms)


def shards(a_vals, a_cols, a_count, p_vals, p_mask):
    rows_here = a_cols.shape[0]
    slot_count = a_cols.shape[1]
    block_size = a_vals.shape[1]
    prol_slots = p_mask.shape[1]
    group_total = lax.axis_size("rows") * lax.axis_size("cols")
    position = lax.axis_index("rows") * lax.axis_size("cols") + lax.axis_index("cols")
    flat_axis = ("rows", "cols")
    slot_ids = jnp.arange(prol_slots, dtype=jnp.int32)
    target = position + slot_ids - 2
    inside = ((target >= 0) & (target < group_total)).astype(jnp.float32)
    keep = jnp.repeat(p_mask.astype(jnp.float32) * inside[None, :], block_size, axis=1)
    pflat = p_vals * keep[:, None, :]
    lower_rows = from_behind(pflat, flat_axis, 1)
    upper_rows = from_behind(pflat, flat_axis, -1)
    span = rows_here * block_size
    width = prol_slots * block_size
    p_own = pflat.reshape(span, width)

    local_cols = a_cols - (position - 1) * rows_here
    live_mask = jnp.arange(slot_count, dtype=jnp.int32)[None, :] < a_count[:, None]
    col_ids = jnp.arange(3 * rows_here, dtype=jnp.int32)
    hit = live_mask[:, :, None] & (local_cols[:, :, None] == col_ids[None, None, :])
    slot_numbers = jnp.arange(1, slot_count + 1, dtype=jnp.int32)[None, :, None]
    slot_table = (jnp.sum(jnp.where(hit, slot_numbers, 0), axis=1) - 1).reshape(-1)
    dense = [side.reshape(span, span) for side in dense_sides(slot_table, a_vals)]

    def pt_times(side):
        return lax.dot_general(
            p_own,
            dense[side],
            (((0,), (0,)), ((), ())),
            precision=MATMUL_PRECISION,
            preferred_element_type=jnp.float32,
        )

    t_own = mm(pt_times(1), p_own)
    t_low = mm(pt_times(0), lower_rows.reshape(span, width))
    t_high = mm(pt_times(2), upper_rows.reshape(span, width))
    terms = (
        jnp.pad(t_low, ((0, 0), (0, 2 * block_size)))
        + jnp.pad(t_own, ((0, 0), (block_size, block_size)))
        + jnp.pad(t_high, ((0, 0), (2 * block_size, 0)))
    ).reshape(prol_slots, block_size, (prol_slots + 2) * block_size)

    def spread(s, block):
        return jnp.pad(block, ((0, 0), ((prol_slots - 1 - s) * block_size, s * block_size)))

    arrived = exchange(terms)
    result = spread(2, terms[2])
    for u, s in enumerate([0, 1, 3, 4]):
        result = result + spread(s, arrived[u])
    return result.reshape(1, block_size, (prol_slots + 6) * block_size)


def solution(mesh):
    in_specs = (
        P(("rows", "cols"), None, None),
        P(("rows", "cols"), None),
        P(("rows", "cols")),
        P(("rows", "cols"), None, None),
        P(("rows", "cols"), None),
    )
    out_specs = P(("rows", "cols"), None, None)
    return jax.shard_map(shards, mesh=mesh, in_specs=in_specs, out_specs=out_specs, check_vma=False)
```

```python
import jax
import jax.numpy as jnp
from jax import lax
from jax.experimental import pallas as pl
from jax.experimental.pallas import tpu as pltpu
from jax.sharding import PartitionSpec as P

MATMUL_PRECISION = lax.Precision.HIGH


def from_behind(array, axis, by):
    count = lax.axis_size(axis)
    pairs = [(i, i + by) for i in range(count) if 0 <= i + by < count]
    return lax.ppermute(array, axis, pairs)


def mm(a, b):
    return jnp.dot(a, b, precision=MATMUL_PRECISION, preferred_element_type=jnp.float32)


CHUNKS = 4


CHUNKS = 4


def dense_kernel(slot_ref, a_ref, *out_refs):
    sides = len(out_refs)
    rows_here, block_size, span = out_refs[0].shape
    per_side = span // block_size
    lanes = 2 * block_size
    left = lax.broadcasted_iota(jnp.int32, (block_size, lanes), 1) < block_size

    def one_row(i, carry):
        for d in range(sides):
            for m in range(per_side // 2):
                halves = []
                for h in range(2):
                    slot = slot_ref[(i * sides + d) * per_side + 2 * m + h]
                    safe = jnp.maximum(slot, 0)
                    start = pl.multiple_of((safe // 2) * lanes, lanes)
                    tile = a_ref[i, :, pl.ds(start, lanes)]
                    rolled = pltpu.roll(tile, block_size, 1)
                    turn = (safe % 2) != h
                    picked = jnp.where(turn, rolled, tile)
                    halves.append(jnp.where(slot >= 0, picked, jnp.zeros_like(picked)))
                out_refs[d][i, :, m * lanes : (m + 1) * lanes] = jnp.where(left, halves[0], halves[1])
        return carry

    lax.fori_loop(0, rows_here, one_row, 0)


def dense_sides(slot_table, a_vals):
    rows_here, block_size, _ = a_vals.shape
    span = rows_here * block_size
    return pl.pallas_call(
        dense_kernel,
        out_shape=[jax.ShapeDtypeStruct((rows_here, block_size, span), jnp.float32)] * 3,
        in_specs=[
            pl.BlockSpec(memory_space=pltpu.SMEM),
            pl.BlockSpec(memory_space=pltpu.VMEM),
        ],
        out_specs=[pl.BlockSpec(memory_space=pltpu.VMEM)] * 3,
    )(slot_table, a_vals)


def neighbour_kernel(p_ref, lower_ref, upper_ref, landed, send_sem, recv_sem):
    col_count = lax.axis_size("cols")
    total = lax.axis_size("rows") * col_count
    me = lax.axis_index("rows") * col_count + lax.axis_index("cols")
    chunk = p_ref.shape[0] // CHUNKS
    routes = [(1, 0), (-1, 1)]
    barrier = pltpu.get_barrier_semaphore()
    peers = 0
    for shift, _ in routes:
        there = (me + shift >= 0) & (me + shift < total)
        peers = peers + there.astype(jnp.int32)

        @pl.when(there)
        def _():
            pl.semaphore_signal(
                barrier,
                1,
                device_id=((me + shift) // col_count, (me + shift) % col_count),
                device_id_type=pl.DeviceIdType.MESH,
            )

    pl.semaphore_wait(barrier, peers)
    copies = []
    for c in range(CHUNKS):
        for shift, slot in routes:
            there = (me + shift >= 0) & (me + shift < total)
            rows = pl.ds(c * chunk, chunk)
            copy = pltpu.make_async_remote_copy(
                src_ref=p_ref.at[rows],
                dst_ref=landed.at[slot, rows],
                send_sem=send_sem.at[slot * CHUNKS + c],
                recv_sem=recv_sem.at[slot * CHUNKS + c],
                device_id=((me + shift) // col_count, (me + shift) % col_count),
                device_id_type=pl.DeviceIdType.MESH,
            )
            copies.append((shift, slot, c, copy))

            @pl.when(there)
            def _():
                copy.start()

    for shift, slot, c, copy in copies:
        sends = (me + shift >= 0) & (me + shift < total)
        gets = (me - shift >= 0) & (me - shift < total)
        target = (lower_ref, upper_ref)[slot]
        rows = pl.ds(c * chunk, chunk)

        @pl.when(sends)
        def _():
            copy.wait_send()

        @pl.when(gets)
        def _():
            copy.wait_recv()
            target[rows] = landed[slot, rows]

        @pl.when(jnp.logical_not(gets))
        def _():
            target[rows] = jnp.zeros(target[rows].shape, target.dtype)


def neighbours(p_rows):
    return pl.pallas_call(
        neighbour_kernel,
        out_shape=[jax.ShapeDtypeStruct(p_rows.shape, jnp.float32)] * 2,
        in_specs=[pl.BlockSpec(memory_space=pltpu.VMEM)],
        out_specs=[pl.BlockSpec(memory_space=pltpu.VMEM)] * 2,
        scratch_shapes=[
            pltpu.VMEM((2,) + p_rows.shape, jnp.float32),
            pltpu.SemaphoreType.DMA((2 * CHUNKS,)),
            pltpu.SemaphoreType.DMA((2 * CHUNKS,)),
        ],
        compiler_params=pltpu.CompilerParams(collective_id=1, has_side_effects=True),
    )(p_rows)


def exchange_kernel(terms_ref, out_ref, recv, send_sem, recv_sem):
    col_count = lax.axis_size("cols")
    total = lax.axis_size("rows") * col_count
    me = lax.axis_index("rows") * col_count + lax.axis_index("cols")
    centre = terms_ref.shape[0] // 2
    shifts = [s - centre for s in range(terms_ref.shape[0]) if s != centre]

    def mesh_id(pos):
        return (pos // col_count, pos % col_count)

    barrier = pltpu.get_barrier_semaphore()
    for shift in shifts:
        @pl.when((me + shift >= 0) & (me + shift < total))
        def _():
            pl.semaphore_signal(
                barrier, 1, device_id=mesh_id(me + shift), device_id_type=pl.DeviceIdType.MESH
            )

    peers = 0
    for shift in shifts:
        peers = peers + ((me + shift >= 0) & (me + shift < total)).astype(jnp.int32)
    pl.semaphore_wait(barrier, peers)

    copies = []
    for u, shift in enumerate(shifts):
        copy = pltpu.make_async_remote_copy(
            src_ref=terms_ref.at[shift + centre],
            dst_ref=recv.at[u],
            send_sem=send_sem.at[u],
            recv_sem=recv_sem.at[u],
            device_id=mesh_id(me + shift),
            device_id_type=pl.DeviceIdType.MESH,
        )
        copies.append(copy)

        @pl.when((me + shift >= 0) & (me + shift < total))
        def _():
            copy.start()

    for u, shift in enumerate(shifts):
        sends = (me + shift >= 0) & (me + shift < total)
        gets = (me - shift >= 0) & (me - shift < total)

        @pl.when(sends)
        def _():
            copies[u].wait_send()

        @pl.when(gets)
        def _():
            copies[u].wait_recv()
            out_ref[u] = recv[u]

        @pl.when(jnp.logical_not(gets))
        def _():
            out_ref[u] = jnp.zeros(out_ref.shape[1:], out_ref.dtype)


def exchange(terms):
    parts, block_size, wide = terms.shape
    return pl.pallas_call(
        exchange_kernel,
        out_shape=jax.ShapeDtypeStruct((parts - 1, block_size, wide), jnp.float32),
        in_specs=[pl.BlockSpec(memory_space=pltpu.VMEM)],
        out_specs=pl.BlockSpec(memory_space=pltpu.VMEM),
        scratch_shapes=[
            pltpu.VMEM((parts - 1, block_size, wide), jnp.float32),
            pltpu.SemaphoreType.DMA((parts - 1,)),
            pltpu.SemaphoreType.DMA((parts - 1,)),
        ],
        compiler_params=pltpu.CompilerParams(collective_id=0, has_side_effects=True),
    )(terms)


def shards(a_vals, a_cols, a_count, p_vals, p_mask):
    rows_here = a_cols.shape[0]
    slot_count = a_cols.shape[1]
    block_size = a_vals.shape[1]
    prol_slots = p_mask.shape[1]
    group_total = lax.axis_size("rows") * lax.axis_size("cols")
    position = lax.axis_index("rows") * lax.axis_size("cols") + lax.axis_index("cols")
    flat_axis = ("rows", "cols")
    slot_ids = jnp.arange(prol_slots, dtype=jnp.int32)
    target = position + slot_ids - 2
    inside = ((target >= 0) & (target < group_total)).astype(jnp.float32)
    keep = jnp.repeat(p_mask.astype(jnp.float32) * inside[None, :], block_size, axis=1)
    pflat = p_vals * keep[:, None, :]
    span = rows_here * block_size
    width = prol_slots * block_size
    p_own = pflat.reshape(span, width)

    local_cols = a_cols - (position - 1) * rows_here
    live_mask = jnp.arange(slot_count, dtype=jnp.int32)[None, :] < a_count[:, None]
    col_ids = jnp.arange(3 * rows_here, dtype=jnp.int32)
    hit = live_mask[:, :, None] & (local_cols[:, :, None] == col_ids[None, None, :])
    slot_numbers = jnp.arange(1, slot_count + 1, dtype=jnp.int32)[None, :, None]
    slot_table = (jnp.sum(jnp.where(hit, slot_numbers, 0), axis=1) - 1).reshape(-1)
    dense = [side.reshape(span, span) for side in dense_sides(slot_table, a_vals)]
    lower_rows, upper_rows = neighbours(pflat)

    def pt_times(side):
        return lax.dot_general(
            p_own,
            dense[side],
            (((0,), (0,)), ((), ())),
            precision=MATMUL_PRECISION,
            preferred_element_type=jnp.float32,
        )

    t_own = mm(pt_times(1), p_own)
    t_low = mm(pt_times(0), lower_rows.reshape(span, width))
    t_high = mm(pt_times(2), upper_rows.reshape(span, width))
    terms = (
        jnp.pad(t_low, ((0, 0), (0, 2 * block_size)))
        + jnp.pad(t_own, ((0, 0), (block_size, block_size)))
        + jnp.pad(t_high, ((0, 0), (2 * block_size, 0)))
    ).reshape(prol_slots, block_size, (prol_slots + 2) * block_size)

    def spread(s, block):
        return jnp.pad(block, ((0, 0), ((prol_slots - 1 - s) * block_size, s * block_size)))

    arrived = exchange(terms)
    result = spread(2, terms[2])
    for u, s in enumerate([0, 1, 3, 4]):
        result = result + spread(s, arrived[u])
    return result.reshape(1, block_size, (prol_slots + 6) * block_size)


def solution(mesh):
    in_specs = (
        P(("rows", "cols"), None, None),
        P(("rows", "cols"), None),
        P(("rows", "cols")),
        P(("rows", "cols"), None, None),
        P(("rows", "cols"), None),
    )
    out_specs = P(("rows", "cols"), None, None)
    return jax.shard_map(shards, mesh=mesh, in_specs=in_specs, out_specs=out_specs, check_vma=False)
```

```python
import jax
import jax.numpy as jnp
from jax import lax
from jax.experimental import pallas as pl
from jax.experimental.pallas import tpu as pltpu
from jax.sharding import PartitionSpec as P

MATMUL_PRECISION = lax.Precision.HIGH


def from_behind(array, axis, by):
    count = lax.axis_size(axis)
    pairs = [(i, i + by) for i in range(count) if 0 <= i + by < count]
    return lax.ppermute(array, axis, pairs)


def mm(a, b):
    return jnp.dot(a, b, precision=MATMUL_PRECISION, preferred_element_type=jnp.float32)


def dense_kernel(slot_ref, a_ref, *out_refs):
    sides = len(out_refs)
    rows_here, block_size, span = out_refs[0].shape
    per_side = span // block_size
    lanes = 2 * block_size
    left = lax.broadcasted_iota(jnp.int32, (block_size, lanes), 1) < block_size

    def one_row(i, carry):
        for d in range(sides):
            for m in range(per_side // 2):
                halves = []
                for h in range(2):
                    slot = slot_ref[(i * sides + d) * per_side + 2 * m + h]
                    safe = jnp.maximum(slot, 0)
                    start = pl.multiple_of((safe // 2) * lanes, lanes)
                    tile = a_ref[i, :, pl.ds(start, lanes)]
                    rolled = pltpu.roll(tile, block_size, 1)
                    turn = (safe % 2) != h
                    picked = jnp.where(turn, rolled, tile)
                    halves.append(jnp.where(slot >= 0, picked, jnp.zeros_like(picked)))
                out_refs[d][i, :, m * lanes : (m + 1) * lanes] = jnp.where(left, halves[0], halves[1])
        return carry

    lax.fori_loop(0, rows_here, one_row, 0)


def dense_sides(slot_table, a_vals):
    rows_here, block_size, _ = a_vals.shape
    span = rows_here * block_size
    return pl.pallas_call(
        dense_kernel,
        out_shape=[jax.ShapeDtypeStruct((rows_here, block_size, span), jnp.float32)] * 3,
        in_specs=[
            pl.BlockSpec(memory_space=pltpu.SMEM),
            pl.BlockSpec(memory_space=pltpu.VMEM),
        ],
        out_specs=[pl.BlockSpec(memory_space=pltpu.VMEM)] * 3,
    )(slot_table, a_vals)


def shards(a_vals, a_cols, a_count, p_vals, p_mask):
    rows_here = a_cols.shape[0]
    slot_count = a_cols.shape[1]
    block_size = a_vals.shape[1]
    prol_slots = p_mask.shape[1]
    group_total = lax.axis_size("rows") * lax.axis_size("cols")
    position = lax.axis_index("rows") * lax.axis_size("cols") + lax.axis_index("cols")
    flat_axis = ("rows", "cols")
    slot_ids = jnp.arange(prol_slots, dtype=jnp.int32)
    target = position + slot_ids - 2
    inside = ((target >= 0) & (target < group_total)).astype(jnp.float32)
    keep = jnp.repeat(p_mask.astype(jnp.float32) * inside[None, :], block_size, axis=1)
    pflat = p_vals * keep[:, None, :]
    lower_rows = from_behind(pflat, flat_axis, 1)
    upper_rows = from_behind(pflat, flat_axis, -1)
    span = rows_here * block_size
    width = prol_slots * block_size
    p_own = pflat.reshape(span, width)

    local_cols = a_cols - (position - 1) * rows_here
    live_mask = jnp.arange(slot_count, dtype=jnp.int32)[None, :] < a_count[:, None]
    col_ids = jnp.arange(3 * rows_here, dtype=jnp.int32)
    hit = live_mask[:, :, None] & (local_cols[:, :, None] == col_ids[None, None, :])
    slot_numbers = jnp.arange(1, slot_count + 1, dtype=jnp.int32)[None, :, None]
    slot_table = (jnp.sum(jnp.where(hit, slot_numbers, 0), axis=1) - 1).reshape(-1)
    dense = [side.reshape(span, span) for side in dense_sides(slot_table, a_vals)]

    def pt_times(side):
        return lax.dot_general(
            p_own,
            dense[side],
            (((0,), (0,)), ((), ())),
            precision=MATMUL_PRECISION,
            preferred_element_type=jnp.float32,
        )

    t_own = mm(pt_times(1), p_own)
    t_low = mm(pt_times(0), lower_rows.reshape(span, width))
    t_high = mm(pt_times(2), upper_rows.reshape(span, width))
    terms = (
        jnp.pad(t_low, ((0, 0), (0, 2 * block_size)))
        + jnp.pad(t_own, ((0, 0), (block_size, block_size)))
        + jnp.pad(t_high, ((0, 0), (2 * block_size, 0)))
    ).reshape(prol_slots, block_size, (prol_slots + 2) * block_size)

    def spread(s, block):
        return jnp.pad(block, ((0, 0), ((prol_slots - 1 - s) * block_size, s * block_size)))

    result = spread(2, terms[2])
    result = result + spread(0, from_behind(terms[0], flat_axis, -2))
    result = result + spread(1, from_behind(terms[1], flat_axis, -1))
    result = result + spread(4, from_behind(terms[4], flat_axis, 2))
    result = result + spread(3, from_behind(terms[3], flat_axis, 1))
    return result.reshape(1, block_size, (prol_slots + 6) * block_size)


def solution(mesh):
    in_specs = (
        P(("rows", "cols"), None, None),
        P(("rows", "cols"), None),
        P(("rows", "cols")),
        P(("rows", "cols"), None, None),
        P(("rows", "cols"), None),
    )
    out_specs = P(("rows", "cols"), None, None)
    return jax.shard_map(shards, mesh=mesh, in_specs=in_specs, out_specs=out_specs, check_vma=False)
```

```python
import jax
import jax.numpy as jnp
from jax import lax
from jax.experimental import pallas as pl
from jax.experimental.pallas import tpu as pltpu
from jax.sharding import PartitionSpec as P

MATMUL_PRECISION = lax.Precision.HIGH


def from_behind(array, axis, by):
    count = lax.axis_size(axis)
    pairs = [(i, i + by) for i in range(count) if 0 <= i + by < count]
    return lax.ppermute(array, axis, pairs)


def mm(a, b):
    return jnp.dot(a, b, precision=MATMUL_PRECISION, preferred_element_type=jnp.float32)


def dense_kernel(slot_ref, a_ref, *out_refs):
    sides = len(out_refs)
    rows_here, block_size, span = out_refs[0].shape
    per_side = span // block_size
    lanes = 2 * block_size
    left = lax.broadcasted_iota(jnp.int32, (block_size, lanes), 1) < block_size

    def one_row(i, carry):
        for d in range(sides):
            for m in range(per_side // 2):
                halves = []
                for h in range(2):
                    slot = slot_ref[(i * sides + d) * per_side + 2 * m + h]
                    safe = jnp.maximum(slot, 0)
                    start = pl.multiple_of((safe // 2) * lanes, lanes)
                    tile = a_ref[i, :, pl.ds(start, lanes)]
                    rolled = pltpu.roll(tile, block_size, 1)
                    turn = (safe % 2) != h
                    picked = jnp.where(turn, rolled, tile)
                    halves.append(jnp.where(slot >= 0, picked, jnp.zeros_like(picked)))
                out_refs[d][i, :, m * lanes : (m + 1) * lanes] = jnp.where(left, halves[0], halves[1])
        return carry

    lax.fori_loop(0, rows_here, one_row, 0)


def dense_sides(slot_table, a_vals):
    rows_here, block_size, _ = a_vals.shape
    span = rows_here * block_size
    return pl.pallas_call(
        dense_kernel,
        out_shape=[jax.ShapeDtypeStruct((rows_here, block_size, span), jnp.float32)] * 3,
        in_specs=[
            pl.BlockSpec(memory_space=pltpu.SMEM),
            pl.BlockSpec(memory_space=pltpu.VMEM),
        ],
        out_specs=[pl.BlockSpec(memory_space=pltpu.VMEM)] * 3,
    )(slot_table, a_vals)


def shards(a_vals, a_cols, a_count, p_vals, p_mask):
    rows_here = a_cols.shape[0]
    slot_count = a_cols.shape[1]
    block_size = a_vals.shape[1]
    prol_slots = p_mask.shape[1]
    group_total = lax.axis_size("rows") * lax.axis_size("cols")
    position = lax.axis_index("rows") * lax.axis_size("cols") + lax.axis_index("cols")
    flat_axis = ("rows", "cols")
    slot_ids = jnp.arange(prol_slots, dtype=jnp.int32)
    target = position + slot_ids - 2
    inside = ((target >= 0) & (target < group_total)).astype(jnp.float32)
    keep = jnp.repeat(p_mask.astype(jnp.float32) * inside[None, :], block_size, axis=1)
    pflat = p_vals * keep[:, None, :]
    lower_rows = from_behind(pflat, flat_axis, 1)
    upper_rows = from_behind(pflat, flat_axis, -1)
    span = rows_here * block_size
    width = prol_slots * block_size
    p_own = pflat.reshape(span, width)

    local_cols = a_cols - (position - 1) * rows_here
    live_mask = jnp.arange(slot_count, dtype=jnp.int32)[None, :] < a_count[:, None]
    col_ids = jnp.arange(3 * rows_here, dtype=jnp.int32)
    hit = live_mask[:, :, None] & (local_cols[:, :, None] == col_ids[None, None, :])
    slot_numbers = jnp.arange(1, slot_count + 1, dtype=jnp.int32)[None, :, None]
    slot_table = (jnp.sum(jnp.where(hit, slot_numbers, 0), axis=1) - 1).reshape(-1)
    dense = [side.reshape(span, span) for side in dense_sides(slot_table, a_vals)]

    def pt_times(side):
        return lax.dot_general(
            p_own,
            dense[side],
            (((0,), (0,)), ((), ())),
            precision=MATMUL_PRECISION,
            preferred_element_type=jnp.float32,
        )

    t_own = mm(pt_times(1), p_own)
    t_high = mm(pt_times(2), upper_rows.reshape(span, width))
    early = (
        jnp.pad(t_own, ((0, 0), (block_size, block_size)))
        + jnp.pad(t_high, ((0, 0), (2 * block_size, 0)))
    ).reshape(prol_slots, block_size, (prol_slots + 2) * block_size)
    sent = [from_behind(early[s], flat_axis, s - 2) for s in (3, 4, 1, 0)]
    lower_rows, sent, early = lax.optimization_barrier((lower_rows, sent, early))
    late = mm(pt_times(0), lower_rows.reshape(span, width)).reshape(prol_slots, block_size, width)

    def spread(s, block):
        left = (prol_slots - 1 - s) * block_size
        right = (prol_slots + 6) * block_size - left - block.shape[1]
        return jnp.pad(block, ((0, 0), (left, right)))

    result = spread(2, early[2]) + spread(2, late[2])
    for s, arrived in zip((3, 4, 1, 0), sent):
        result = result + spread(s, arrived)
    for s in (3, 4, 1, 0):
        result = result + spread(s, from_behind(late[s], flat_axis, s - 2))
    return result.reshape(1, block_size, (prol_slots + 6) * block_size)


def solution(mesh):
    in_specs = (
        P(("rows", "cols"), None, None),
        P(("rows", "cols"), None),
        P(("rows", "cols")),
        P(("rows", "cols"), None, None),
        P(("rows", "cols"), None),
    )
    out_specs = P(("rows", "cols"), None, None)
    return jax.shard_map(shards, mesh=mesh, in_specs=in_specs, out_specs=out_specs, check_vma=False)
```

```python
import jax
import jax.numpy as jnp
from jax import lax
from jax.experimental import pallas as pl
from jax.experimental.pallas import tpu as pltpu
from jax.sharding import PartitionSpec as P

MATMUL_PRECISION = lax.Precision.HIGH


def from_behind(array, axis, by):
    count = lax.axis_size(axis)
    pairs = [(i, i + by) for i in range(count) if 0 <= i + by < count]
    return lax.ppermute(array, axis, pairs)


def mm(a, b):
    return jnp.dot(a, b, precision=MATMUL_PRECISION, preferred_element_type=jnp.float32)


def dense_kernel(slot_ref, a_ref, *out_refs):
    sides = len(out_refs)
    rows_here, block_size, span = out_refs[0].shape
    per_side = span // block_size
    lanes = 2 * block_size
    left = lax.broadcasted_iota(jnp.int32, (block_size, lanes), 1) < block_size

    def one_row(i, carry):
        for d in range(sides):
            for m in range(per_side // 2):
                halves = []
                for h in range(2):
                    slot = slot_ref[(i * sides + d) * per_side + 2 * m + h]
                    safe = jnp.maximum(slot, 0)
                    start = pl.multiple_of((safe // 2) * lanes, lanes)
                    tile = a_ref[i, :, pl.ds(start, lanes)]
                    rolled = pltpu.roll(tile, block_size, 1)
                    turn = (safe % 2) != h
                    picked = jnp.where(turn, rolled, tile)
                    halves.append(jnp.where(slot >= 0, picked, jnp.zeros_like(picked)))
                out_refs[d][i, :, m * lanes : (m + 1) * lanes] = jnp.where(left, halves[0], halves[1])
        return carry

    lax.fori_loop(0, rows_here, one_row, 0)


def dense_sides(slot_table, a_vals):
    rows_here, block_size, _ = a_vals.shape
    span = rows_here * block_size
    return pl.pallas_call(
        dense_kernel,
        out_shape=[jax.ShapeDtypeStruct((rows_here, block_size, span), jnp.float32)] * 3,
        in_specs=[
            pl.BlockSpec(memory_space=pltpu.SMEM),
            pl.BlockSpec(memory_space=pltpu.VMEM),
        ],
        out_specs=[pl.BlockSpec(memory_space=pltpu.VMEM)] * 3,
    )(slot_table, a_vals)


def exchange_kernel(terms_ref, out_ref, recv, acc, padded, send_sem, recv_sem):
    col_count = lax.axis_size("cols")
    total = lax.axis_size("rows") * col_count
    me = lax.axis_index("rows") * col_count + lax.axis_index("cols")
    centre = terms_ref.shape[0] // 2
    shifts = [s - centre for s in range(terms_ref.shape[0]) if s != centre]

    def mesh_id(pos):
        return (pos // col_count, pos % col_count)

    barrier = pltpu.get_barrier_semaphore()
    for shift in shifts:
        @pl.when((me + shift >= 0) & (me + shift < total))
        def _():
            pl.semaphore_signal(
                barrier, 1, device_id=mesh_id(me + shift), device_id_type=pl.DeviceIdType.MESH
            )

    peers = 0
    for shift in shifts:
        peers = peers + ((me + shift >= 0) & (me + shift < total)).astype(jnp.int32)
    pl.semaphore_wait(barrier, peers)

    copies = []
    for u, shift in enumerate(shifts):
        copy = pltpu.make_async_remote_copy(
            src_ref=terms_ref.at[shift + centre],
            dst_ref=recv.at[u],
            send_sem=send_sem.at[u],
            recv_sem=recv_sem.at[u],
            device_id=mesh_id(me + shift),
            device_id_type=pl.DeviceIdType.MESH,
        )
        copies.append(copy)

        @pl.when((me + shift >= 0) & (me + shift < total))
        def _():
            copy.start()

    block_size = terms_ref.shape[1]
    lanes = 2 * block_size
    acc[...] = jnp.zeros(acc.shape, acc.dtype)

    def place(part_ref, offset):
        wide = part_ref.shape[-1]
        if offset % lanes == 0:
            acc[:, offset : offset + wide] += part_ref[...]
        else:
            padded[...] = jnp.zeros(padded.shape, padded.dtype)
            padded[:, :wide] = part_ref[...]
            base = offset - block_size
            acc[:, base : base + padded.shape[1]] += pltpu.roll(padded[...], block_size, 1)

    place(terms_ref.at[centre], centre * block_size)
    for u, shift in enumerate(shifts):
        sends = (me + shift >= 0) & (me + shift < total)
        gets = (me - shift >= 0) & (me - shift < total)

        @pl.when(sends)
        def _():
            copies[u].wait_send()

        @pl.when(gets)
        def _():
            copies[u].wait_recv()
            place(recv.at[u], (centre - shift) * block_size)

    out_ref[...] = acc[:, : out_ref.shape[1]]


def exchange(terms):
    parts, block_size, wide = terms.shape
    lanes = 2 * block_size
    full = wide + (parts - 1) * block_size
    return pl.pallas_call(
        exchange_kernel,
        out_shape=jax.ShapeDtypeStruct((block_size, full), jnp.float32),
        in_specs=[pl.BlockSpec(memory_space=pltpu.VMEM)],
        out_specs=pl.BlockSpec(memory_space=pltpu.VMEM),
        scratch_shapes=[
            pltpu.VMEM((parts - 1, block_size, wide), jnp.float32),
            pltpu.VMEM((block_size, -(-full // lanes) * lanes), jnp.float32),
            pltpu.VMEM((block_size, -(-wide // lanes) * lanes), jnp.float32),
            pltpu.SemaphoreType.DMA((parts - 1,)),
            pltpu.SemaphoreType.DMA((parts - 1,)),
        ],
        compiler_params=pltpu.CompilerParams(collective_id=0, has_side_effects=True),
    )(terms)


def shards(a_vals, a_cols, a_count, p_vals, p_mask):
    rows_here = a_cols.shape[0]
    slot_count = a_cols.shape[1]
    block_size = a_vals.shape[1]
    prol_slots = p_mask.shape[1]
    group_total = lax.axis_size("rows") * lax.axis_size("cols")
    position = lax.axis_index("rows") * lax.axis_size("cols") + lax.axis_index("cols")
    flat_axis = ("rows", "cols")
    slot_ids = jnp.arange(prol_slots, dtype=jnp.int32)
    target = position + slot_ids - 2
    inside = ((target >= 0) & (target < group_total)).astype(jnp.float32)
    keep = jnp.repeat(p_mask.astype(jnp.float32) * inside[None, :], block_size, axis=1)
    pflat = p_vals * keep[:, None, :]
    lower_rows = from_behind(pflat, flat_axis, 1)
    upper_rows = from_behind(pflat, flat_axis, -1)
    span = rows_here * block_size
    width = prol_slots * block_size
    p_own = pflat.reshape(span, width)

    local_cols = a_cols - (position - 1) * rows_here
    live_mask = jnp.arange(slot_count, dtype=jnp.int32)[None, :] < a_count[:, None]
    col_ids = jnp.arange(3 * rows_here, dtype=jnp.int32)
    hit = live_mask[:, :, None] & (local_cols[:, :, None] == col_ids[None, None, :])
    slot_numbers = jnp.arange(1, slot_count + 1, dtype=jnp.int32)[None, :, None]
    slot_table = (jnp.sum(jnp.where(hit, slot_numbers, 0), axis=1) - 1).reshape(-1)
    dense = [side.reshape(span, span) for side in dense_sides(slot_table, a_vals)]

    def pt_times(side):
        return lax.dot_general(
            p_own,
            dense[side],
            (((0,), (0,)), ((), ())),
            precision=MATMUL_PRECISION,
            preferred_element_type=jnp.float32,
        )

    t_own = mm(pt_times(1), p_own)
    t_low = mm(pt_times(0), lower_rows.reshape(span, width))
    t_high = mm(pt_times(2), upper_rows.reshape(span, width))
    terms = (
        jnp.pad(t_low, ((0, 0), (0, 2 * block_size)))
        + jnp.pad(t_own, ((0, 0), (block_size, block_size)))
        + jnp.pad(t_high, ((0, 0), (2 * block_size, 0)))
    ).reshape(prol_slots, block_size, (prol_slots + 2) * block_size)

    result = exchange(terms)
    return result.reshape(1, block_size, (prol_slots + 6) * block_size)


def solution(mesh):
    in_specs = (
        P(("rows", "cols"), None, None),
        P(("rows", "cols"), None),
        P(("rows", "cols")),
        P(("rows", "cols"), None, None),
        P(("rows", "cols"), None),
    )
    out_specs = P(("rows", "cols"), None, None)
    return jax.shard_map(shards, mesh=mesh, in_specs=in_specs, out_specs=out_specs, check_vma=False)
```

```python
import jax
import jax.numpy as jnp
from jax import lax
from jax.experimental import pallas as pl
from jax.experimental.pallas import tpu as pltpu
from jax.sharding import PartitionSpec as P

MATMUL_PRECISION = lax.Precision.HIGH


def from_behind(array, axis, by):
    count = lax.axis_size(axis)
    pairs = [(i, i + by) for i in range(count) if 0 <= i + by < count]
    return lax.ppermute(array, axis, pairs)


def mm(a, b):
    return jnp.dot(a, b, precision=MATMUL_PRECISION, preferred_element_type=jnp.float32)


def dense_kernel(slot_ref, a_ref, *out_refs):
    sides = len(out_refs)
    rows_here, block_size, span = out_refs[0].shape
    per_side = span // block_size
    lanes = 2 * block_size
    left = lax.broadcasted_iota(jnp.int32, (block_size, lanes), 1) < block_size

    def one_row(i, carry):
        for d in range(sides):
            for m in range(per_side // 2):
                halves = []
                for h in range(2):
                    slot = slot_ref[(i * sides + d) * per_side + 2 * m + h]
                    safe = jnp.maximum(slot, 0)
                    start = pl.multiple_of((safe // 2) * lanes, lanes)
                    tile = a_ref[i, :, pl.ds(start, lanes)]
                    rolled = pltpu.roll(tile, block_size, 1)
                    turn = (safe % 2) != h
                    picked = jnp.where(turn, rolled, tile)
                    halves.append(jnp.where(slot >= 0, picked, jnp.zeros_like(picked)))
                out_refs[d][i, :, m * lanes : (m + 1) * lanes] = jnp.where(left, halves[0], halves[1])
        return carry

    lax.fori_loop(0, rows_here, one_row, 0)


def dense_sides(slot_table, a_vals):
    rows_here, block_size, _ = a_vals.shape
    span = rows_here * block_size
    return pl.pallas_call(
        dense_kernel,
        out_shape=[jax.ShapeDtypeStruct((rows_here, block_size, span), jnp.float32)] * 3,
        in_specs=[
            pl.BlockSpec(memory_space=pltpu.SMEM),
            pl.BlockSpec(memory_space=pltpu.VMEM),
        ],
        out_specs=[pl.BlockSpec(memory_space=pltpu.VMEM)] * 3,
    )(slot_table, a_vals)


def exchange_kernel(terms_ref, out_ref, land1, bufs_r, bufs_l, land_r, land_l, acc, padded, sems):
    col_count = lax.axis_size("cols")
    total = lax.axis_size("rows") * col_count
    me = lax.axis_index("rows") * col_count + lax.axis_index("cols")
    block_size = terms_ref.shape[1]
    lanes = 2 * block_size
    has = {1: me + 1 < total, -1: me - 1 >= 0}

    def mesh_id(pos):
        return (pos // col_count, pos % col_count)

    def place(target, part, offset):
        wide = part.shape[-1]
        if offset % lanes == 0:
            target[:, offset : offset + wide] += part
        else:
            padded[...] = jnp.zeros(padded.shape, padded.dtype)
            padded[:, :wide] = part
            base = offset - block_size
            target[:, base : base + padded.shape[1]] += pltpu.roll(padded[...], block_size, 1)

    barrier = pltpu.get_barrier_semaphore()
    for shift in (1, -1):
        @pl.when(has[shift])
        def _():
            pl.semaphore_signal(
                barrier, 1, device_id=mesh_id(me + shift), device_id_type=pl.DeviceIdType.MESH
            )

    pl.semaphore_wait(barrier, has[1].astype(jnp.int32) + has[-1].astype(jnp.int32))

    def remote(src, dst, k, shift):
        return pltpu.make_async_remote_copy(
            src_ref=src,
            dst_ref=dst,
            send_sem=sems.at[0, k],
            recv_sem=sems.at[1, k],
            device_id=mesh_id(me + shift),
            device_id_type=pl.DeviceIdType.MESH,
        )

    first = [remote(terms_ref.at[4], land1.at[0], 0, 1), remote(terms_ref.at[0], land1.at[1], 1, -1)]
    for copy, shift in zip(first, (1, -1)):
        @pl.when(has[shift])
        def _():
            copy.start()

    bufs_r[...] = jnp.zeros(bufs_r.shape, bufs_r.dtype)
    bufs_l[...] = jnp.zeros(bufs_l.shape, bufs_l.dtype)
    place(bufs_r, terms_ref[3], block_size)
    place(bufs_l, terms_ref[1], block_size)
    for copy, shift, k in zip(first, (1, -1), (0, 1)):
        @pl.when(has[shift])
        def _():
            copy.wait_send()

        @pl.when(has[-shift])
        def _():
            copy.wait_recv()
            if k == 0:
                place(bufs_r, land1[0], 0)
            else:
                place(bufs_l, land1[1], lanes)

    second = [remote(bufs_r, land_r, 2, 1), remote(bufs_l, land_l, 3, -1)]
    for copy, shift in zip(second, (1, -1)):
        @pl.when(has[shift])
        def _():
            copy.start()

    acc[...] = jnp.zeros(acc.shape, acc.dtype)
    place(acc, terms_ref[2], lanes)
    for copy, shift, k in zip(second, (1, -1), (0, 1)):
        @pl.when(has[shift])
        def _():
            copy.wait_send()

        @pl.when(has[-shift])
        def _():
            copy.wait_recv()
            if k == 0:
                acc[:, : land_r.shape[1]] += land_r[...]
            else:
                acc[:, lanes : lanes + land_l.shape[1]] += land_l[...]

    out_ref[...] = acc[:, : out_ref.shape[1]]


def exchange(terms):
    parts, block_size, wide = terms.shape
    lanes = 2 * block_size
    full = wide + (parts - 1) * block_size
    return pl.pallas_call(
        exchange_kernel,
        out_shape=jax.ShapeDtypeStruct((block_size, full), jnp.float32),
        in_specs=[pl.BlockSpec(memory_space=pltpu.VMEM)],
        out_specs=pl.BlockSpec(memory_space=pltpu.VMEM),
        scratch_shapes=[
            pltpu.VMEM((2, block_size, wide), jnp.float32),
            pltpu.VMEM((block_size, wide + block_size), jnp.float32),
            pltpu.VMEM((block_size, wide + lanes), jnp.float32),
            pltpu.VMEM((block_size, wide + block_size), jnp.float32),
            pltpu.VMEM((block_size, wide + lanes), jnp.float32),
            pltpu.VMEM((block_size, -(-full // lanes) * lanes), jnp.float32),
            pltpu.VMEM((block_size, -(-wide // lanes) * lanes), jnp.float32),
            pltpu.SemaphoreType.DMA((2, 4)),
        ],
        compiler_params=pltpu.CompilerParams(collective_id=0, has_side_effects=True),
    )(terms)


def shards(a_vals, a_cols, a_count, p_vals, p_mask):
    rows_here = a_cols.shape[0]
    slot_count = a_cols.shape[1]
    block_size = a_vals.shape[1]
    prol_slots = p_mask.shape[1]
    group_total = lax.axis_size("rows") * lax.axis_size("cols")
    position = lax.axis_index("rows") * lax.axis_size("cols") + lax.axis_index("cols")
    flat_axis = ("rows", "cols")
    slot_ids = jnp.arange(prol_slots, dtype=jnp.int32)
    target = position + slot_ids - 2
    inside = ((target >= 0) & (target < group_total)).astype(jnp.float32)
    keep = jnp.repeat(p_mask.astype(jnp.float32) * inside[None, :], block_size, axis=1)
    pflat = p_vals * keep[:, None, :]
    lower_rows = from_behind(pflat, flat_axis, 1)
    upper_rows = from_behind(pflat, flat_axis, -1)
    span = rows_here * block_size
    width = prol_slots * block_size
    p_own = pflat.reshape(span, width)

    local_cols = a_cols - (position - 1) * rows_here
    live_mask = jnp.arange(slot_count, dtype=jnp.int32)[None, :] < a_count[:, None]
    col_ids = jnp.arange(3 * rows_here, dtype=jnp.int32)
    hit = live_mask[:, :, None] & (local_cols[:, :, None] == col_ids[None, None, :])
    slot_numbers = jnp.arange(1, slot_count + 1, dtype=jnp.int32)[None, :, None]
    slot_table = (jnp.sum(jnp.where(hit, slot_numbers, 0), axis=1) - 1).reshape(-1)
    dense = [side.reshape(span, span) for side in dense_sides(slot_table, a_vals)]

    def pt_times(side):
        return lax.dot_general(
            p_own,
            dense[side],
            (((0,), (0,)), ((), ())),
            precision=MATMUL_PRECISION,
            preferred_element_type=jnp.float32,
        )

    t_own = mm(pt_times(1), p_own)
    t_low = mm(pt_times(0), lower_rows.reshape(span, width))
    t_high = mm(pt_times(2), upper_rows.reshape(span, width))
    terms = (
        jnp.pad(t_low, ((0, 0), (0, 2 * block_size)))
        + jnp.pad(t_own, ((0, 0), (block_size, block_size)))
        + jnp.pad(t_high, ((0, 0), (2 * block_size, 0)))
    ).reshape(prol_slots, block_size, (prol_slots + 2) * block_size)

    result = exchange(terms)
    return result.reshape(1, block_size, (prol_slots + 6) * block_size)


def solution(mesh):
    in_specs = (
        P(("rows", "cols"), None, None),
        P(("rows", "cols"), None),
        P(("rows", "cols")),
        P(("rows", "cols"), None, None),
        P(("rows", "cols"), None),
    )
    out_specs = P(("rows", "cols"), None, None)
    return jax.shard_map(shards, mesh=mesh, in_specs=in_specs, out_specs=out_specs, check_vma=False)
```

```python
import jax
import jax.numpy as jnp
from jax import lax
from jax.experimental import pallas as pl
from jax.experimental.pallas import tpu as pltpu
from jax.sharding import PartitionSpec as P

MATMUL_PRECISION = lax.Precision.HIGH


def from_behind(array, axis, by):
    count = lax.axis_size(axis)
    pairs = [(i, i + by) for i in range(count) if 0 <= i + by < count]
    return lax.ppermute(array, axis, pairs)


def mm(a, b):
    return jnp.dot(a, b, precision=MATMUL_PRECISION, preferred_element_type=jnp.float32)


def dense_kernel(slot_ref, a_ref, *out_refs):
    sides = len(out_refs)
    rows_here, block_size, span = out_refs[0].shape
    per_side = span // block_size
    lanes = 2 * block_size
    left = lax.broadcasted_iota(jnp.int32, (block_size, lanes), 1) < block_size

    def one_row(i, carry):
        for d in range(sides):
            for m in range(per_side // 2):
                halves = []
                for h in range(2):
                    slot = slot_ref[(i * sides + d) * per_side + 2 * m + h]
                    safe = jnp.maximum(slot, 0)
                    start = pl.multiple_of((safe // 2) * lanes, lanes)
                    tile = a_ref[i, :, pl.ds(start, lanes)]
                    rolled = pltpu.roll(tile, block_size, 1)
                    turn = (safe % 2) != h
                    picked = jnp.where(turn, rolled, tile)
                    halves.append(jnp.where(slot >= 0, picked, jnp.zeros_like(picked)))
                out_refs[d][i, :, m * lanes : (m + 1) * lanes] = jnp.where(left, halves[0], halves[1])
        return carry

    lax.fori_loop(0, rows_here, one_row, 0)


def dense_sides(slot_table, a_vals):
    rows_here, block_size, _ = a_vals.shape
    span = rows_here * block_size
    return pl.pallas_call(
        dense_kernel,
        out_shape=[jax.ShapeDtypeStruct((rows_here, block_size, span), jnp.float32)] * 3,
        in_specs=[
            pl.BlockSpec(memory_space=pltpu.SMEM),
            pl.BlockSpec(memory_space=pltpu.VMEM),
        ],
        out_specs=[pl.BlockSpec(memory_space=pltpu.VMEM)] * 3,
    )(slot_table, a_vals)


def shards(a_vals, a_cols, a_count, p_vals, p_mask):
    rows_here = a_cols.shape[0]
    slot_count = a_cols.shape[1]
    block_size = a_vals.shape[1]
    prol_slots = p_mask.shape[1]
    group_total = lax.axis_size("rows") * lax.axis_size("cols")
    position = lax.axis_index("rows") * lax.axis_size("cols") + lax.axis_index("cols")
    flat_axis = ("rows", "cols")
    lower_raw, lower_mask = from_behind((p_vals, p_mask), flat_axis, 1)
    upper_raw, upper_mask = from_behind((p_vals, p_mask), flat_axis, -1)
    slot_ids = jnp.arange(prol_slots, dtype=jnp.int32)

    def keep_of(mask, owner):
        target = owner + slot_ids - 2
        inside = ((target >= 0) & (target < group_total)).astype(jnp.float32)
        return jnp.repeat(mask.astype(jnp.float32) * inside[None, :], block_size, axis=1)[:, None, :]

    pflat = p_vals * keep_of(p_mask, position)
    lower_rows = lower_raw * keep_of(lower_mask, position - 1)
    upper_rows = upper_raw * keep_of(upper_mask, position + 1)
    span = rows_here * block_size
    width = prol_slots * block_size
    p_own = pflat.reshape(span, width)

    local_cols = a_cols - (position - 1) * rows_here
    live_mask = jnp.arange(slot_count, dtype=jnp.int32)[None, :] < a_count[:, None]
    col_ids = jnp.arange(3 * rows_here, dtype=jnp.int32)
    hit = live_mask[:, :, None] & (local_cols[:, :, None] == col_ids[None, None, :])
    slot_numbers = jnp.arange(1, slot_count + 1, dtype=jnp.int32)[None, :, None]
    slot_table = (jnp.sum(jnp.where(hit, slot_numbers, 0), axis=1) - 1).reshape(-1)
    dense = [side.reshape(span, span) for side in dense_sides(slot_table, a_vals)]

    def pt_times(side):
        return lax.dot_general(
            p_own,
            dense[side],
            (((0,), (0,)), ((), ())),
            precision=MATMUL_PRECISION,
            preferred_element_type=jnp.float32,
        )

    t_own = mm(pt_times(1), p_own)
    t_low = mm(pt_times(0), lower_rows.reshape(span, width))
    t_high = mm(pt_times(2), upper_rows.reshape(span, width))
    terms = (
        jnp.pad(t_low, ((0, 0), (0, 2 * block_size)))
        + jnp.pad(t_own, ((0, 0), (block_size, block_size)))
        + jnp.pad(t_high, ((0, 0), (2 * block_size, 0)))
    ).reshape(prol_slots, block_size, (prol_slots + 2) * block_size)

    def spread(s, block):
        return jnp.pad(block, ((0, 0), ((prol_slots - 1 - s) * block_size, s * block_size)))

    result = spread(2, terms[2])
    result = result + spread(3, from_behind(terms[3], flat_axis, 1))
    result = result + spread(4, from_behind(terms[4], flat_axis, 2))
    result = result + spread(1, from_behind(terms[1], flat_axis, -1))
    result = result + spread(0, from_behind(terms[0], flat_axis, -2))
    return result.reshape(1, block_size, (prol_slots + 6) * block_size)


def solution(mesh):
    in_specs = (
        P(("rows", "cols"), None, None),
        P(("rows", "cols"), None),
        P(("rows", "cols")),
        P(("rows", "cols"), None, None),
        P(("rows", "cols"), None),
    )
    out_specs = P(("rows", "cols"), None, None)
    return jax.shard_map(shards, mesh=mesh, in_specs=in_specs, out_specs=out_specs, check_vma=False)
```

```python
import jax
import jax.numpy as jnp
from jax import lax
from jax.experimental import pallas as pl
from jax.experimental.pallas import tpu as pltpu
from jax.sharding import PartitionSpec as P

MATMUL_PRECISION = lax.Precision.HIGH


def from_behind(array, axis, by):
    count = lax.axis_size(axis)
    pairs = [(i, i + by) for i in range(count) if 0 <= i + by < count]
    return lax.ppermute(array, axis, pairs)


def mm(a, b):
    return jnp.dot(a, b, precision=MATMUL_PRECISION, preferred_element_type=jnp.float32)


def dense_kernel(slot_ref, a_ref, *out_refs):
    sides = len(out_refs)
    rows_here, block_size, span = out_refs[0].shape
    per_side = span // block_size
    lanes = 2 * block_size
    left = lax.broadcasted_iota(jnp.int32, (block_size, lanes), 1) < block_size

    def one_row(i, carry):
        for d in range(sides):
            for m in range(per_side // 2):
                halves = []
                for h in range(2):
                    slot = slot_ref[(i * sides + d) * per_side + 2 * m + h]
                    safe = jnp.maximum(slot, 0)
                    start = pl.multiple_of((safe // 2) * lanes, lanes)
                    tile = a_ref[i, :, pl.ds(start, lanes)]
                    rolled = pltpu.roll(tile, block_size, 1)
                    turn = (safe % 2) != h
                    picked = jnp.where(turn, rolled, tile)
                    halves.append(jnp.where(slot >= 0, picked, jnp.zeros_like(picked)))
                out_refs[d][i, :, m * lanes : (m + 1) * lanes] = jnp.where(left, halves[0], halves[1])
        return carry

    lax.fori_loop(0, rows_here, one_row, 0)


def dense_sides(slot_table, a_vals):
    rows_here, block_size, _ = a_vals.shape
    span = rows_here * block_size
    return pl.pallas_call(
        dense_kernel,
        out_shape=[jax.ShapeDtypeStruct((rows_here, block_size, span), jnp.float32)] * 3,
        in_specs=[
            pl.BlockSpec(memory_space=pltpu.SMEM),
            pl.BlockSpec(memory_space=pltpu.VMEM),
        ],
        out_specs=[pl.BlockSpec(memory_space=pltpu.VMEM)] * 3,
    )(slot_table, a_vals)


def exchange_kernel(terms_ref, out_ref, land1, bufs_r, bufs_l, land_r, land_l, acc, padded, sems):
    col_count = lax.axis_size("cols")
    total = lax.axis_size("rows") * col_count
    me = lax.axis_index("rows") * col_count + lax.axis_index("cols")
    block_size = terms_ref.shape[1]
    lanes = 2 * block_size
    has = {1: me + 1 < total, -1: me - 1 >= 0}

    def mesh_id(pos):
        return (pos // col_count, pos % col_count)

    def place(target, part, offset):
        wide = part.shape[-1]
        if offset % lanes == 0:
            target[:, offset : offset + wide] += part
        else:
            padded[...] = jnp.zeros(padded.shape, padded.dtype)
            padded[:, :wide] = part
            base = offset - block_size
            target[:, base : base + padded.shape[1]] += pltpu.roll(padded[...], block_size, 1)

    barrier = pltpu.get_barrier_semaphore()
    for shift in (1, -1):
        @pl.when(has[shift])
        def _():
            pl.semaphore_signal(
                barrier, 1, device_id=mesh_id(me + shift), device_id_type=pl.DeviceIdType.MESH
            )

    pl.semaphore_wait(barrier, has[1].astype(jnp.int32) + has[-1].astype(jnp.int32))

    def remote(src, dst, k, shift):
        return pltpu.make_async_remote_copy(
            src_ref=src,
            dst_ref=dst,
            send_sem=sems.at[0, k],
            recv_sem=sems.at[1, k],
            device_id=mesh_id(me + shift),
            device_id_type=pl.DeviceIdType.MESH,
        )

    first = [remote(terms_ref.at[4], land1.at[0], 0, 1), remote(terms_ref.at[0], land1.at[1], 1, -1)]
    for copy, shift in zip(first, (1, -1)):
        @pl.when(has[shift])
        def _():
            copy.start()

    bufs_r[...] = jnp.zeros(bufs_r.shape, bufs_r.dtype)
    bufs_l[...] = jnp.zeros(bufs_l.shape, bufs_l.dtype)
    place(bufs_r, terms_ref[3], block_size)
    place(bufs_l, terms_ref[1], block_size)
    for copy, shift, k in zip(first, (1, -1), (0, 1)):
        @pl.when(has[shift])
        def _():
            copy.wait_send()

        @pl.when(has[-shift])
        def _():
            copy.wait_recv()
            if k == 0:
                place(bufs_r, land1[0], 0)
            else:
                place(bufs_l, land1[1], lanes)

    second = [remote(bufs_r, land_r, 2, 1), remote(bufs_l, land_l, 3, -1)]
    for copy, shift in zip(second, (1, -1)):
        @pl.when(has[shift])
        def _():
            copy.start()

    acc[...] = jnp.zeros(acc.shape, acc.dtype)
    for copy, shift, k in zip(second, (1, -1), (0, 1)):
        @pl.when(has[shift])
        def _():
            copy.wait_send()

        @pl.when(has[-shift])
        def _():
            copy.wait_recv()
            if k == 0:
                acc[:, : land_r.shape[1]] += land_r[...]
            else:
                acc[:, lanes : lanes + land_l.shape[1]] += land_l[...]

    out_ref[...] = acc[:, : out_ref.shape[1]]


def exchange(terms):
    parts, block_size, wide = terms.shape
    lanes = 2 * block_size
    full = wide + (parts - 1) * block_size
    return pl.pallas_call(
        exchange_kernel,
        out_shape=jax.ShapeDtypeStruct((block_size, full), jnp.float32),
        in_specs=[pl.BlockSpec(memory_space=pltpu.VMEM)],
        out_specs=pl.BlockSpec(memory_space=pltpu.VMEM),
        scratch_shapes=[
            pltpu.VMEM((2, block_size, wide), jnp.float32),
            pltpu.VMEM((block_size, wide + block_size), jnp.float32),
            pltpu.VMEM((block_size, wide + lanes), jnp.float32),
            pltpu.VMEM((block_size, wide + block_size), jnp.float32),
            pltpu.VMEM((block_size, wide + lanes), jnp.float32),
            pltpu.VMEM((block_size, -(-full // lanes) * lanes), jnp.float32),
            pltpu.VMEM((block_size, -(-wide // lanes) * lanes), jnp.float32),
            pltpu.SemaphoreType.DMA((2, 4)),
        ],
        compiler_params=pltpu.CompilerParams(collective_id=0, has_side_effects=True),
    )(terms)


def shards(a_vals, a_cols, a_count, p_vals, p_mask):
    rows_here = a_cols.shape[0]
    slot_count = a_cols.shape[1]
    block_size = a_vals.shape[1]
    prol_slots = p_mask.shape[1]
    group_total = lax.axis_size("rows") * lax.axis_size("cols")
    position = lax.axis_index("rows") * lax.axis_size("cols") + lax.axis_index("cols")
    flat_axis = ("rows", "cols")
    slot_ids = jnp.arange(prol_slots, dtype=jnp.int32)
    target = position + slot_ids - 2
    inside = ((target >= 0) & (target < group_total)).astype(jnp.float32)
    keep = jnp.repeat(p_mask.astype(jnp.float32) * inside[None, :], block_size, axis=1)
    pflat = p_vals * keep[:, None, :]
    lower_rows = from_behind(pflat, flat_axis, 1)
    upper_rows = from_behind(pflat, flat_axis, -1)
    span = rows_here * block_size
    width = prol_slots * block_size
    p_own = pflat.reshape(span, width)

    local_cols = a_cols - (position - 1) * rows_here
    live_mask = jnp.arange(slot_count, dtype=jnp.int32)[None, :] < a_count[:, None]
    col_ids = jnp.arange(3 * rows_here, dtype=jnp.int32)
    hit = live_mask[:, :, None] & (local_cols[:, :, None] == col_ids[None, None, :])
    slot_numbers = jnp.arange(1, slot_count + 1, dtype=jnp.int32)[None, :, None]
    slot_table = (jnp.sum(jnp.where(hit, slot_numbers, 0), axis=1) - 1).reshape(-1)
    dense = [side.reshape(span, span) for side in dense_sides(slot_table, a_vals)]

    def pt_times(side):
        return lax.dot_general(
            p_own,
            dense[side],
            (((0,), (0,)), ((), ())),
            precision=MATMUL_PRECISION,
            preferred_element_type=jnp.float32,
        )

    t_own = mm(pt_times(1), p_own)
    t_low = mm(pt_times(0), lower_rows.reshape(span, width))
    t_high = mm(pt_times(2), upper_rows.reshape(span, width))
    terms = (
        jnp.pad(t_low, ((0, 0), (0, 2 * block_size)))
        + jnp.pad(t_own, ((0, 0), (block_size, block_size)))
        + jnp.pad(t_high, ((0, 0), (2 * block_size, 0)))
    ).reshape(prol_slots, block_size, (prol_slots + 2) * block_size)

    result = exchange(terms) + jnp.pad(terms[2], ((0, 0), (2 * block_size, 2 * block_size)))
    return result.reshape(1, block_size, (prol_slots + 6) * block_size)


def solution(mesh):
    in_specs = (
        P(("rows", "cols"), None, None),
        P(("rows", "cols"), None),
        P(("rows", "cols")),
        P(("rows", "cols"), None, None),
        P(("rows", "cols"), None),
    )
    out_specs = P(("rows", "cols"), None, None)
    return jax.shard_map(shards, mesh=mesh, in_specs=in_specs, out_specs=out_specs, check_vma=False)
```

```python
import jax
import jax.numpy as jnp
from jax import lax
from jax.experimental import pallas as pl
from jax.experimental.pallas import tpu as pltpu
from jax.sharding import PartitionSpec as P

MATMUL_PRECISION = lax.Precision.HIGH


def from_behind(array, axis, by):
    count = lax.axis_size(axis)
    pairs = [(i, i + by) for i in range(count) if 0 <= i + by < count]
    return lax.ppermute(array, axis, pairs)


def mm(a, b):
    return jnp.dot(a, b, precision=MATMUL_PRECISION, preferred_element_type=jnp.float32)


def dense_kernel(slot_ref, a_ref, *out_refs):
    sides = len(out_refs)
    rows_here, block_size, span = out_refs[0].shape
    per_side = span // block_size
    lanes = 2 * block_size
    left = lax.broadcasted_iota(jnp.int32, (block_size, lanes), 1) < block_size

    def one_row(i, carry):
        for d in range(sides):
            for m in range(per_side // 2):
                halves = []
                for h in range(2):
                    slot = slot_ref[(i * sides + d) * per_side + 2 * m + h]
                    safe = jnp.maximum(slot, 0)
                    start = pl.multiple_of((safe // 2) * lanes, lanes)
                    tile = a_ref[i, :, pl.ds(start, lanes)]
                    rolled = pltpu.roll(tile, block_size, 1)
                    turn = (safe % 2) != h
                    picked = jnp.where(turn, rolled, tile)
                    halves.append(jnp.where(slot >= 0, picked, jnp.zeros_like(picked)))
                out_refs[d][i, :, m * lanes : (m + 1) * lanes] = jnp.where(left, halves[0], halves[1])
        return carry

    lax.fori_loop(0, rows_here, one_row, 0)


def dense_sides(slot_table, a_vals):
    rows_here, block_size, _ = a_vals.shape
    span = rows_here * block_size
    return pl.pallas_call(
        dense_kernel,
        out_shape=[jax.ShapeDtypeStruct((rows_here, block_size, span), jnp.float32)] * 3,
        in_specs=[
            pl.BlockSpec(memory_space=pltpu.SMEM),
            pl.BlockSpec(memory_space=pltpu.VMEM),
        ],
        out_specs=[pl.BlockSpec(memory_space=pltpu.VMEM)] * 3,
    )(slot_table, a_vals)


def exchange_kernel(
    terms_ref, out_ref, land1, bufs_r, bufs_l, send_r, send_l, land_r, land_l, acc, padded, sems, local_sems
):
    col_count = lax.axis_size("cols")
    total = lax.axis_size("rows") * col_count
    me = lax.axis_index("rows") * col_count + lax.axis_index("cols")
    block_size = terms_ref.shape[1]
    lanes = 2 * block_size
    has = {1: me + 1 < total, -1: me - 1 >= 0}

    def mesh_id(pos):
        return (pos // col_count, pos % col_count)

    def place(target, part, offset):
        wide = part.shape[-1]
        if offset % lanes == 0:
            target[:, offset : offset + wide] += part
        else:
            padded[...] = jnp.zeros(padded.shape, padded.dtype)
            padded[:, :wide] = part
            base = offset - block_size
            target[:, base : base + padded.shape[1]] += pltpu.roll(padded[...], block_size, 1)

    barrier = pltpu.get_barrier_semaphore()
    for shift in (1, -1):
        @pl.when(has[shift])
        def _():
            pl.semaphore_signal(
                barrier, 1, device_id=mesh_id(me + shift), device_id_type=pl.DeviceIdType.MESH
            )

    pl.semaphore_wait(barrier, has[1].astype(jnp.int32) + has[-1].astype(jnp.int32))

    def remote(src, dst, k, shift):
        return pltpu.make_async_remote_copy(
            src_ref=src,
            dst_ref=dst,
            send_sem=sems.at[0, k],
            recv_sem=sems.at[1, k],
            device_id=mesh_id(me + shift),
            device_id_type=pl.DeviceIdType.MESH,
        )

    first = [remote(terms_ref.at[4], land1.at[0], 0, 1), remote(terms_ref.at[0], land1.at[1], 1, -1)]
    for copy, shift in zip(first, (1, -1)):
        @pl.when(has[shift])
        def _():
            copy.start()

    bufs_r[...] = jnp.zeros(bufs_r.shape, bufs_r.dtype)
    bufs_l[...] = jnp.zeros(bufs_l.shape, bufs_l.dtype)
    place(bufs_r, terms_ref[3], block_size)
    place(bufs_l, terms_ref[1], block_size)
    for copy, shift, k in zip(first, (1, -1), (0, 1)):
        @pl.when(has[shift])
        def _():
            copy.wait_send()

        @pl.when(has[-shift])
        def _():
            copy.wait_recv()
            if k == 0:
                place(bufs_r, land1[0], 0)
            else:
                place(bufs_l, land1[1], lanes)

    staged = [
        pltpu.make_async_copy(bufs_r, send_r, local_sems.at[0]),
        pltpu.make_async_copy(bufs_l, send_l, local_sems.at[1]),
    ]
    for copy in staged:
        copy.start()
    for copy in staged:
        copy.wait()
    second = [remote(send_r, land_r, 2, 1), remote(send_l, land_l, 3, -1)]
    for copy, shift in zip(second, (1, -1)):
        @pl.when(has[shift])
        def _():
            copy.start()

    acc[...] = jnp.zeros(acc.shape, acc.dtype)
    for copy, shift, k in zip(second, (1, -1), (0, 1)):
        @pl.when(has[shift])
        def _():
            copy.wait_send()

        @pl.when(has[-shift])
        def _():
            copy.wait_recv()
            if k == 0:
                acc[:, : land_r.shape[1]] += land_r[...]
            else:
                acc[:, lanes : lanes + land_l.shape[1]] += land_l[...]

    out_ref[...] = acc[:, : out_ref.shape[1]]


def exchange(terms):
    parts, block_size, wide = terms.shape
    lanes = 2 * block_size
    full = wide + (parts - 1) * block_size
    return pl.pallas_call(
        exchange_kernel,
        out_shape=jax.ShapeDtypeStruct((block_size, full), jnp.float32),
        in_specs=[pl.BlockSpec(memory_space=pltpu.VMEM)],
        out_specs=pl.BlockSpec(memory_space=pltpu.VMEM),
        scratch_shapes=[
            pltpu.VMEM((2, block_size, wide), jnp.float32),
            pltpu.VMEM((block_size, wide + block_size), jnp.float32),
            pltpu.VMEM((block_size, wide + lanes), jnp.float32),
            pltpu.VMEM((block_size, wide + block_size), jnp.float32),
            pltpu.VMEM((block_size, wide + lanes), jnp.float32),
            pltpu.VMEM((block_size, wide + block_size), jnp.float32),
            pltpu.VMEM((block_size, wide + lanes), jnp.float32),
            pltpu.VMEM((block_size, -(-full // lanes) * lanes), jnp.float32),
            pltpu.VMEM((block_size, -(-wide // lanes) * lanes), jnp.float32),
            pltpu.SemaphoreType.DMA((2, 4)),
            pltpu.SemaphoreType.DMA((2,)),
        ],
        compiler_params=pltpu.CompilerParams(collective_id=0, has_side_effects=True),
    )(terms)


def shards(a_vals, a_cols, a_count, p_vals, p_mask):
    rows_here = a_cols.shape[0]
    slot_count = a_cols.shape[1]
    block_size = a_vals.shape[1]
    prol_slots = p_mask.shape[1]
    group_total = lax.axis_size("rows") * lax.axis_size("cols")
    position = lax.axis_index("rows") * lax.axis_size("cols") + lax.axis_index("cols")
    flat_axis = ("rows", "cols")
    slot_ids = jnp.arange(prol_slots, dtype=jnp.int32)
    target = position + slot_ids - 2
    inside = ((target >= 0) & (target < group_total)).astype(jnp.float32)
    keep = jnp.repeat(p_mask.astype(jnp.float32) * inside[None, :], block_size, axis=1)
    pflat = p_vals * keep[:, None, :]
    lower_rows = from_behind(pflat, flat_axis, 1)
    upper_rows = from_behind(pflat, flat_axis, -1)
    span = rows_here * block_size
    width = prol_slots * block_size
    p_own = pflat.reshape(span, width)

    local_cols = a_cols - (position - 1) * rows_here
    live_mask = jnp.arange(slot_count, dtype=jnp.int32)[None, :] < a_count[:, None]
    col_ids = jnp.arange(3 * rows_here, dtype=jnp.int32)
    hit = live_mask[:, :, None] & (local_cols[:, :, None] == col_ids[None, None, :])
    slot_numbers = jnp.arange(1, slot_count + 1, dtype=jnp.int32)[None, :, None]
    slot_table = (jnp.sum(jnp.where(hit, slot_numbers, 0), axis=1) - 1).reshape(-1)
    dense = [side.reshape(span, span) for side in dense_sides(slot_table, a_vals)]

    def pt_times(side):
        return lax.dot_general(
            p_own,
            dense[side],
            (((0,), (0,)), ((), ())),
            precision=MATMUL_PRECISION,
            preferred_element_type=jnp.float32,
        )

    t_own = mm(pt_times(1), p_own)
    t_low = mm(pt_times(0), lower_rows.reshape(span, width))
    t_high = mm(pt_times(2), upper_rows.reshape(span, width))
    terms = (
        jnp.pad(t_low, ((0, 0), (0, 2 * block_size)))
        + jnp.pad(t_own, ((0, 0), (block_size, block_size)))
        + jnp.pad(t_high, ((0, 0), (2 * block_size, 0)))
    ).reshape(prol_slots, block_size, (prol_slots + 2) * block_size)

    result = exchange(terms) + jnp.pad(terms[2], ((0, 0), (2 * block_size, 2 * block_size)))
    return result.reshape(1, block_size, (prol_slots + 6) * block_size)


def solution(mesh):
    in_specs = (
        P(("rows", "cols"), None, None),
        P(("rows", "cols"), None),
        P(("rows", "cols")),
        P(("rows", "cols"), None, None),
        P(("rows", "cols"), None),
    )
    out_specs = P(("rows", "cols"), None, None)
    return jax.shard_map(shards, mesh=mesh, in_specs=in_specs, out_specs=out_specs, check_vma=False)
```

```python
import jax
import jax.numpy as jnp
from jax import lax
from jax.experimental import pallas as pl
from jax.experimental.pallas import tpu as pltpu
from jax.sharding import PartitionSpec as P

MATMUL_PRECISION = lax.Precision.HIGH


def from_behind(array, axis, by):
    count = lax.axis_size(axis)
    pairs = [(i, i + by) for i in range(count) if 0 <= i + by < count]
    return lax.ppermute(array, axis, pairs)


def mm(a, b):
    return jnp.dot(a, b, precision=MATMUL_PRECISION, preferred_element_type=jnp.float32)


def dense_kernel(slot_ref, a_ref, *out_refs):
    sides = len(out_refs)
    rows_here, block_size, span = out_refs[0].shape
    per_side = span // block_size
    lanes = 2 * block_size
    left = lax.broadcasted_iota(jnp.int32, (block_size, lanes), 1) < block_size

    def one_row(i, carry):
        for d in range(sides):
            for m in range(per_side // 2):
                halves = []
                for h in range(2):
                    slot = slot_ref[(i * sides + d) * per_side + 2 * m + h]
                    safe = jnp.maximum(slot, 0)
                    start = pl.multiple_of((safe // 2) * lanes, lanes)
                    tile = a_ref[i, :, pl.ds(start, lanes)]
                    rolled = pltpu.roll(tile, block_size, 1)
                    turn = (safe % 2) != h
                    picked = jnp.where(turn, rolled, tile)
                    halves.append(jnp.where(slot >= 0, picked, jnp.zeros_like(picked)))
                out_refs[d][i, :, m * lanes : (m + 1) * lanes] = jnp.where(left, halves[0], halves[1])
        return carry

    lax.fori_loop(0, rows_here, one_row, 0)


def dense_sides(slot_table, a_vals):
    rows_here, block_size, _ = a_vals.shape
    span = rows_here * block_size
    return pl.pallas_call(
        dense_kernel,
        out_shape=[jax.ShapeDtypeStruct((rows_here, block_size, span), jnp.float32)] * 3,
        in_specs=[
            pl.BlockSpec(memory_space=pltpu.SMEM),
            pl.BlockSpec(memory_space=pltpu.VMEM),
        ],
        out_specs=[pl.BlockSpec(memory_space=pltpu.VMEM)] * 3,
    )(slot_table, a_vals)


def shards(a_vals, a_cols, a_count, p_vals, p_mask):
    rows_here = a_cols.shape[0]
    slot_count = a_cols.shape[1]
    block_size = a_vals.shape[1]
    prol_slots = p_mask.shape[1]
    group_total = lax.axis_size("rows") * lax.axis_size("cols")
    position = lax.axis_index("rows") * lax.axis_size("cols") + lax.axis_index("cols")
    flat_axis = ("rows", "cols")
    slot_ids = jnp.arange(prol_slots, dtype=jnp.int32)
    target = position + slot_ids - 2
    inside = ((target >= 0) & (target < group_total)).astype(jnp.float32)
    keep = jnp.repeat(p_mask.astype(jnp.float32) * inside[None, :], block_size, axis=1)
    pflat = p_vals * keep[:, None, :]
    lower_rows = from_behind(pflat, flat_axis, 1)
    upper_rows = from_behind(pflat, flat_axis, -1)
    span = rows_here * block_size
    width = prol_slots * block_size
    p_own = pflat.reshape(span, width)

    local_cols = a_cols - (position - 1) * rows_here
    live_mask = jnp.arange(slot_count, dtype=jnp.int32)[None, :] < a_count[:, None]
    col_ids = jnp.arange(3 * rows_here, dtype=jnp.int32)
    hit = live_mask[:, :, None] & (local_cols[:, :, None] == col_ids[None, None, :])
    slot_numbers = jnp.arange(1, slot_count + 1, dtype=jnp.int32)[None, :, None]
    slot_table = (jnp.sum(jnp.where(hit, slot_numbers, 0), axis=1) - 1).reshape(-1)
    dense = [side.reshape(span, span) for side in dense_sides(slot_table, a_vals)]

    def pt_times(side):
        return lax.dot_general(
            p_own,
            dense[side],
            (((0,), (0,)), ((), ())),
            precision=MATMUL_PRECISION,
            preferred_element_type=jnp.float32,
        )

    t_own = mm(pt_times(1), p_own)
    t_low = mm(pt_times(0), lower_rows.reshape(span, width))
    partial = jnp.pad(t_low, ((0, 0), (0, 2 * block_size))) + jnp.pad(t_own, ((0, 0), (block_size, block_size)))
    partial, high_w = lax.optimization_barrier((partial, pt_times(2)))
    t_high = mm(high_w, upper_rows.reshape(span, width))
    terms = (partial + jnp.pad(t_high, ((0, 0), (2 * block_size, 0)))).reshape(
        prol_slots, block_size, (prol_slots + 2) * block_size
    )

    def spread(s, block):
        return jnp.pad(block, ((0, 0), ((prol_slots - 1 - s) * block_size, s * block_size)))

    result = spread(2, terms[2])
    result = result + spread(3, from_behind(terms[3], flat_axis, 1))
    result = result + spread(4, from_behind(terms[4], flat_axis, 2))
    result = result + spread(1, from_behind(terms[1], flat_axis, -1))
    result = result + spread(0, from_behind(terms[0], flat_axis, -2))
    return result.reshape(1, block_size, (prol_slots + 6) * block_size)


def solution(mesh):
    in_specs = (
        P(("rows", "cols"), None, None),
        P(("rows", "cols"), None),
        P(("rows", "cols")),
        P(("rows", "cols"), None, None),
        P(("rows", "cols"), None),
    )
    out_specs = P(("rows", "cols"), None, None)
    return jax.shard_map(shards, mesh=mesh, in_specs=in_specs, out_specs=out_specs, check_vma=False)
```

```python
import jax
import jax.numpy as jnp
from jax import lax
from jax.experimental import pallas as pl
from jax.experimental.pallas import tpu as pltpu
from jax.sharding import PartitionSpec as P

MATMUL_PRECISION = lax.Precision.HIGH


def from_behind(array, axis, by):
    count = lax.axis_size(axis)
    pairs = [(i, i + by) for i in range(count) if 0 <= i + by < count]
    return lax.ppermute(array, axis, pairs)


def mm(a, b):
    return jnp.dot(a, b, precision=MATMUL_PRECISION, preferred_element_type=jnp.float32)


def dense_kernel(slot_ref, a_ref, *out_refs):
    sides = len(out_refs)
    rows_here, block_size, span = out_refs[0].shape
    per_side = span // block_size
    lanes = 2 * block_size
    left = lax.broadcasted_iota(jnp.int32, (block_size, lanes), 1) < block_size

    def one_row(i, carry):
        for d in range(sides):
            for m in range(per_side // 2):
                halves = []
                for h in range(2):
                    slot = slot_ref[(i * sides + d) * per_side + 2 * m + h]
                    safe = jnp.maximum(slot, 0)
                    start = pl.multiple_of((safe // 2) * lanes, lanes)
                    tile = a_ref[i, :, pl.ds(start, lanes)]
                    rolled = pltpu.roll(tile, block_size, 1)
                    turn = (safe % 2) != h
                    picked = jnp.where(turn, rolled, tile)
                    halves.append(jnp.where(slot >= 0, picked, jnp.zeros_like(picked)))
                out_refs[d][i, :, m * lanes : (m + 1) * lanes] = jnp.where(left, halves[0], halves[1])
        return carry

    lax.fori_loop(0, rows_here, one_row, 0)


def dense_sides(slot_table, a_vals):
    rows_here, block_size, _ = a_vals.shape
    span = rows_here * block_size
    return pl.pallas_call(
        dense_kernel,
        out_shape=[jax.ShapeDtypeStruct((rows_here, block_size, span), jnp.float32)] * 3,
        in_specs=[
            pl.BlockSpec(memory_space=pltpu.SMEM),
            pl.BlockSpec(memory_space=pltpu.VMEM),
        ],
        out_specs=[pl.BlockSpec(memory_space=pltpu.VMEM)] * 3,
    )(slot_table, a_vals)


def exchange_kernel(
    terms_ref, out_ref, land1, bufs_r, bufs_l, send_r, send_l, land_r, land_l, acc, padded, sems, local_sems
):
    col_count = lax.axis_size("cols")
    total = lax.axis_size("rows") * col_count
    me = lax.axis_index("rows") * col_count + lax.axis_index("cols")
    block_size = terms_ref.shape[1]
    lanes = 2 * block_size
    has = {1: me + 1 < total, -1: me - 1 >= 0}

    def mesh_id(pos):
        return (pos // col_count, pos % col_count)

    def place(target, part, offset):
        wide = part.shape[-1]
        if offset % lanes == 0:
            target[:, offset : offset + wide] += part
        else:
            padded[...] = jnp.zeros(padded.shape, padded.dtype)
            padded[:, :wide] = part
            base = offset - block_size
            target[:, base : base + padded.shape[1]] += pltpu.roll(padded[...], block_size, 1)

    barrier = pltpu.get_barrier_semaphore()
    for shift in (1, -1):
        @pl.when(has[shift])
        def _():
            pl.semaphore_signal(
                barrier, 1, device_id=mesh_id(me + shift), device_id_type=pl.DeviceIdType.MESH
            )

    pl.semaphore_wait(barrier, has[1].astype(jnp.int32) + has[-1].astype(jnp.int32))

    def remote(src, dst, k, shift):
        return pltpu.make_async_remote_copy(
            src_ref=src,
            dst_ref=dst,
            send_sem=sems.at[0, k],
            recv_sem=sems.at[1, k],
            device_id=mesh_id(me + shift),
            device_id_type=pl.DeviceIdType.MESH,
        )

    first = [remote(terms_ref.at[4], land1.at[0], 0, 1), remote(terms_ref.at[0], land1.at[1], 1, -1)]
    for copy, shift in zip(first, (1, -1)):
        @pl.when(has[shift])
        def _():
            copy.start()

    bufs_r[...] = jnp.zeros(bufs_r.shape, bufs_r.dtype)
    bufs_l[...] = jnp.zeros(bufs_l.shape, bufs_l.dtype)
    place(bufs_r, terms_ref[3], block_size)
    place(bufs_l, terms_ref[1], block_size)
    for copy, shift, k in zip(first, (1, -1), (0, 1)):
        @pl.when(has[shift])
        def _():
            copy.wait_send()

        @pl.when(has[-shift])
        def _():
            copy.wait_recv()
            if k == 0:
                place(bufs_r, land1[0], 0)
            else:
                place(bufs_l, land1[1], lanes)

    staged = [
        pltpu.make_async_copy(bufs_r, send_r, local_sems.at[0]),
        pltpu.make_async_copy(bufs_l, send_l, local_sems.at[1]),
    ]
    for copy in staged:
        copy.start()
    for copy in staged:
        copy.wait()
    second = [remote(send_r, land_r, 2, 1), remote(send_l, land_l, 3, -1)]
    for copy, shift in zip(second, (1, -1)):
        @pl.when(has[shift])
        def _():
            copy.start()

    acc[...] = jnp.zeros(acc.shape, acc.dtype)
    for copy, shift, k in zip(second, (1, -1), (0, 1)):
        @pl.when(has[shift])
        def _():
            copy.wait_send()

        @pl.when(has[-shift])
        def _():
            copy.wait_recv()
            if k == 0:
                acc[:, : land_r.shape[1]] += land_r[...]
            else:
                acc[:, lanes : lanes + land_l.shape[1]] += land_l[...]

    out_ref[...] = acc[:, : out_ref.shape[1]]


def exchange(terms):
    parts, block_size, wide = terms.shape
    lanes = 2 * block_size
    full = wide + (parts - 1) * block_size
    return pl.pallas_call(
        exchange_kernel,
        out_shape=jax.ShapeDtypeStruct((block_size, full), jnp.float32),
        in_specs=[pl.BlockSpec(memory_space=pltpu.VMEM)],
        out_specs=pl.BlockSpec(memory_space=pltpu.VMEM),
        scratch_shapes=[
            pltpu.VMEM((2, block_size, wide), jnp.float32),
            pltpu.VMEM((block_size, wide + block_size), jnp.float32),
            pltpu.VMEM((block_size, wide + lanes), jnp.float32),
            pltpu.VMEM((block_size, wide + block_size), jnp.float32),
            pltpu.VMEM((block_size, wide + lanes), jnp.float32),
            pltpu.VMEM((block_size, wide + block_size), jnp.float32),
            pltpu.VMEM((block_size, wide + lanes), jnp.float32),
            pltpu.VMEM((block_size, -(-full // lanes) * lanes), jnp.float32),
            pltpu.VMEM((block_size, -(-wide // lanes) * lanes), jnp.float32),
            pltpu.SemaphoreType.DMA((2, 4)),
            pltpu.SemaphoreType.DMA((2,)),
        ],
        compiler_params=pltpu.CompilerParams(collective_id=0, has_side_effects=True),
    )(terms)


def shards(a_vals, a_cols, a_count, p_vals, p_mask):
    rows_here = a_cols.shape[0]
    slot_count = a_cols.shape[1]
    block_size = a_vals.shape[1]
    prol_slots = p_mask.shape[1]
    group_total = lax.axis_size("rows") * lax.axis_size("cols")
    position = lax.axis_index("rows") * lax.axis_size("cols") + lax.axis_index("cols")
    flat_axis = ("rows", "cols")
    slot_ids = jnp.arange(prol_slots, dtype=jnp.int32)
    target = position + slot_ids - 2
    inside = ((target >= 0) & (target < group_total)).astype(jnp.float32)
    keep = jnp.repeat(p_mask.astype(jnp.float32) * inside[None, :], block_size, axis=1)
    pflat = p_vals * keep[:, None, :]
    lower_rows = from_behind(pflat, flat_axis, 1)
    upper_rows = from_behind(pflat, flat_axis, -1)
    span = rows_here * block_size
    width = prol_slots * block_size
    p_own = pflat.reshape(span, width)

    local_cols = a_cols - (position - 1) * rows_here
    live_mask = jnp.arange(slot_count, dtype=jnp.int32)[None, :] < a_count[:, None]
    col_ids = jnp.arange(3 * rows_here, dtype=jnp.int32)
    hit = live_mask[:, :, None] & (local_cols[:, :, None] == col_ids[None, None, :])
    slot_numbers = jnp.arange(1, slot_count + 1, dtype=jnp.int32)[None, :, None]
    slot_table = (jnp.sum(jnp.where(hit, slot_numbers, 0), axis=1) - 1).reshape(-1)
    dense = [side.reshape(span, span) for side in dense_sides(slot_table, a_vals)]

    def pt_times(side):
        return lax.dot_general(
            p_own,
            dense[side],
            (((0,), (0,)), ((), ())),
            precision=MATMUL_PRECISION,
            preferred_element_type=jnp.float32,
        )

    t_own = mm(pt_times(1), p_own)
    t_low = mm(pt_times(0), lower_rows.reshape(span, width))
    partial = jnp.pad(t_low, ((0, 0), (0, 2 * block_size))) + jnp.pad(t_own, ((0, 0), (block_size, block_size)))
    partial, high_w = lax.optimization_barrier((partial, pt_times(2)))
    t_high = mm(high_w, upper_rows.reshape(span, width))
    terms = (partial + jnp.pad(t_high, ((0, 0), (2 * block_size, 0)))).reshape(
        prol_slots, block_size, (prol_slots + 2) * block_size
    )

    result = exchange(terms) + jnp.pad(terms[2], ((0, 0), (2 * block_size, 2 * block_size)))
    return result.reshape(1, block_size, (prol_slots + 6) * block_size)


def solution(mesh):
    in_specs = (
        P(("rows", "cols"), None, None),
        P(("rows", "cols"), None),
        P(("rows", "cols")),
        P(("rows", "cols"), None, None),
        P(("rows", "cols"), None),
    )
    out_specs = P(("rows", "cols"), None, None)
    return jax.shard_map(shards, mesh=mesh, in_specs=in_specs, out_specs=out_specs, check_vma=False)
```
